32 devices in a mesh: groups: 2 (over y), chan: 4 (over z), band: 2 (over x), rep: 2 (over core).
Axes of the slice: x: 2, y: 2, z: 4, core: 2. Of those that a mesh axis runs over, the one named last changes fastest.
Arguments:
- state_field: float32 [256, 64, 1024], P(('groups', 'chan'), ('band', 'rep')), parts along dimension 0, may hold values from -6 to 6
- patch_weight: bfloat16 [1024, 1024], P('rep'), may hold values from -0.1875 to 0.1875
- chan_embed: float32 [128, 1024], P('chan'), may hold values from -6 to 6
- query_keys: bfloat16 [1024, 16], replicated, may hold values from -29 to 29
- value_weight: bfloat16 [1024, 1024], P('rep'), may hold values from -0.1875 to 0.1875
- out_weight: bfloat16 [1024, 1024], P('rep'), may hold values from -0.75 to 0.75
- dec_embed: float32 [128, 1024], P('chan'), may hold values from -6 to 6
- dec_weight: bfloat16 [1024, 1024], P('rep'), may hold values from -0.1875 to 0.1875
Outputs:
- forecast: float32 [256, 64, 1024], P(('groups', 'chan'), ('band', 'rep')), parts along dimension 0
The draws below stay inside these ranges and needn't reach their ends.
There are 2 independent parts, one for each index of `groups`. The reference program is written for one: setup_inputs(seed, part) draws one part's arguments, and reference() takes and returns one part's arrays. A program takes and returns all parts, laid end to end along the dimension named above; an argument that names none is the same for every part. Nothing has to cross between parts.
All inputs are finite; a program needn't handle non-finite values.
Results may differ from the reference program's by a relative error of at most 0.034.
The reference program's roundings to bfloat16 on the way (of `coarse`, `patches`, `tokens`, `normed`, `values`, `blended`, `mixed` and `hidden`) count: a program that leaves them out, or rounds other values in their place, can miss the bound.
Values may be sent and summed in bfloat16 or wider, within the bound.
A program may use at most 192 MiB of HBM per device.

```python
import math
import jax
import jax.numpy as jnp
from jax import lax

C = 128
D = 1024
HEADS = 16
HEAD_DIM = 64
PATCH = 32
STRIDE = 16
RIM = 8
COL_PATCH = 64
STEPS = 2
PROWS = 4
ROWS = 64
COLS = 1024
POS = 256


def draw_query_keys(key, part):
    key_one, key_two, key_three = jax.random.split(key, 3)
    normal_part = jnp.clip(jax.random.normal(key_one, (D, HEADS), jnp.float32), -3.0, 3.0)
    lower = 0.3
    upper = 3.0
    scales = jnp.exp(jax.random.uniform(key_two, (HEADS,), jnp.float32, math.log(lower), math.log(upper)))
    chosen = jax.random.randint(key_three, (), 0, HEADS)
    scales = jnp.where(jnp.arange(HEADS) == chosen, upper, scales)
    return (normal_part * scales[None, :] / 32.0).astype(jnp.bfloat16)


def shard_levels(stream_key, extent, shards, least, high):
    level = 1.0
    for dim, shards_of in shards:
        heights = jax.random.uniform(jax.random.fold_in(jax.random.fold_in(stream_key, 6), dim), (shards_of,), jnp.float32, least / len(shards), high / len(shards))
        level = level * jnp.repeat(jnp.exp(heights), extent[dim] // shards_of).reshape((-1,) + (1,) * (len(extent) - 1 - dim))
    return level


def normal_values(rng, extent, scale, bound, cuts=(), kind=jnp.bfloat16):
    entries = jax.random.normal(rng, extent, jnp.float32) * scale
    if len(cuts) > 0:
        entries = shard_levels(rng, extent, cuts, -0.22, 0.18) * entries
    return jnp.clip(entries, min=-bound, max=bound).astype(kind)


def setup_inputs(seed: int = 0, part: int = 0) -> dict:
    splits = jax.random.split(jax.random.key(seed), 9)
    part_keys = jax.random.split(jax.random.fold_in(splits[8], part), 9)
    return {
        "state_field": normal_values(part_keys[0], (C, ROWS, COLS), 1.0, 6.0, ((0, 4), (1, 4)), jnp.float32),
        "patch_weight": normal_values(splits[1], (PATCH * PATCH, D), (PATCH * PATCH) ** -0.5, 0.1875, ((0, 2),)),
        "chan_embed": normal_values(splits[2], (C, D), 1.0, 6.0, ((0, 4),), jnp.float32),
        "query_keys": draw_query_keys(jax.random.fold_in(splits[8], 71), part),
        "value_weight": normal_values(splits[4], (D, D), D ** -0.5, 0.1875, ((0, 2),)),
        "out_weight": normal_values(splits[5], (D, D), (D // 16) ** -0.5, 0.75, ((0, 2),)),
        "dec_embed": normal_values(splits[6], (C, D), 1.0, 6.0, ((0, 4),), jnp.float32),
        "dec_weight": normal_values(splits[7], (D, PATCH * PATCH), D ** -0.5, 0.1875, ((0, 2),)),
    }


def normalize(tokens):
    values = tokens.astype(jnp.float32)
    centre = lax.optimization_barrier(jnp.mean(values, axis=-1, keepdims=True))
    spread = lax.optimization_barrier(jnp.mean(jnp.square(values - centre), axis=-1, keepdims=True))
    return ((values - centre) * lax.rsqrt(spread + 1e-05)).astype(jnp.bfloat16)

def wrap_columns(blocks, margin):
    return jnp.concatenate([blocks[:, :, -margin:], blocks, blocks[:, :, :margin]], axis=2)

def cut_patches(extended, row_count, col_count, stride):
    chans = extended.shape[0]
    blocks = extended.reshape(chans, row_count + 1, stride, col_count + 1, stride)
    blocks = jnp.concatenate([blocks[:, :-1], blocks[:, 1:]], axis=2)
    blocks = jnp.concatenate([blocks[:, :, :, :-1], blocks[:, :, :, 1:]], axis=4)
    blocks = blocks.transpose(0, 1, 3, 2, 4)
    return blocks.reshape(chans, row_count * col_count, 4 * stride * stride)

def lay_patches(pixels, row_count, col_count, stride):
    chans = pixels.shape[0]
    blocks = pixels.reshape(chans, row_count, col_count, 2 * stride, 2 * stride).transpose(0, 1, 3, 2, 4)
    upper = jnp.pad(blocks[:, :, :stride], ((0, 0), (0, 1), (0, 0), (0, 0), (0, 0)))
    lower = jnp.pad(blocks[:, :, stride:], ((0, 0), (1, 0), (0, 0), (0, 0), (0, 0)))
    blocks = upper + lower
    leftward = jnp.pad(blocks[..., :stride], ((0, 0), (0, 0), (0, 0), (0, 1), (0, 0)))
    rightward = jnp.pad(blocks[..., stride:], ((0, 0), (0, 0), (0, 0), (1, 0), (0, 0)))
    blocks = leftward + rightward
    return 0.25 * blocks.reshape(chans, (row_count + 1) * stride, (col_count + 1) * stride)

def fold_columns(owned_rows, margin, width):
    core = owned_rows[:, :, margin:margin + width]
    beyond_right = owned_rows[:, :, margin + width:]
    beyond_left = owned_rows[:, :, :margin]
    core = core + jnp.pad(beyond_right, ((0, 0), (0, 0), (0, width - margin)))
    return core + jnp.pad(beyond_left, ((0, 0), (0, 0), (width - margin, 0)))

def reference(state_field, patch_weight, chan_embed, query_keys, value_weight, out_weight, dec_embed, dec_weight):
    current = state_field
    for rollout in range(STEPS):
        coarse = current.astype(jnp.bfloat16)
        extended = jnp.pad(coarse, ((0, 0), (RIM, RIM), (0, 0)))
        extended = wrap_columns(extended, RIM)
        patches = cut_patches(extended, PROWS, COL_PATCH, STRIDE)
        embedded = jnp.dot(patches.reshape(C * POS, PATCH * PATCH), patch_weight, preferred_element_type=jnp.float32)
        tokens = (embedded.reshape(C, POS, D) + chan_embed[:, None, :]).astype(jnp.bfloat16)
        normed = normalize(tokens)
        flat = normed.reshape(C * POS, D)
        scores = jnp.dot(flat, query_keys, preferred_element_type=jnp.float32).reshape(C, POS, HEADS)
        weights = jax.nn.softmax(scores, axis=0)
        projected = jnp.dot(flat, value_weight, preferred_element_type=jnp.float32).astype(jnp.bfloat16)
        projected = lax.optimization_barrier(projected)
        values = projected.astype(jnp.float32).reshape(C, POS, HEADS, HEAD_DIM)
        blended = jnp.einsum('cph,cphe->phe', weights, values, precision=lax.Precision.HIGHEST)
        blended = blended.reshape(POS, D).astype(jnp.bfloat16)
        mixed = jnp.dot(blended, out_weight, preferred_element_type=jnp.float32).astype(jnp.bfloat16)
        hidden = jax.nn.gelu(mixed.astype(jnp.float32)[None] + dec_embed[:, None, :], approximate=False).astype(jnp.bfloat16)
        pixels = jnp.dot(hidden.reshape(C * POS, D), dec_weight, preferred_element_type=jnp.float32).reshape(C, POS, PATCH * PATCH)
        canvas = lay_patches(pixels, PROWS, COL_PATCH, STRIDE)
        owned_rows = canvas[:, RIM:RIM + ROWS]
        current = current + fold_columns(owned_rows, RIM, COLS)
    return current
```

```python
import functools

import jax
import jax.numpy as jnp
from jax import lax
from jax.experimental import pallas as pl
from jax.experimental.pallas import tpu as pltpu
from jax.sharding import PartitionSpec as P

D = 1024
HEADS = 16
HEAD_DIM = D // HEADS
PATCH = 32
STRIDE = 16
RIM = 8
STEPS = 2
LANES = 128
COPIES = LANES // HEADS
CHUNK = 16
WIDE = 256
PACKET = D + 2 * LANES
MESH = pl.DeviceIdType.MESH
F32 = jnp.float32
BF16 = jnp.bfloat16


def iota(shape, dim):
    return lax.broadcasted_iota(jnp.int32, shape, dim)


def swap_chunks(tiles):
    tiles = list(tiles)
    chunk = lax.shift_right_logical(iota(tiles[0].shape, 1), 4)
    for bit in (1, 2, 4):
        high = (chunk & bit) != 0
        for low in range(8):
            if low & bit:
                continue
            first, second = tiles[low], tiles[low + bit]
            tiles[low] = jnp.where(high, pltpu.roll(second, 16 * bit, 1), first)
            tiles[low + bit] = jnp.where(high, second, pltpu.roll(first, LANES - 16 * bit, 1))
    return tiles


def split_parts(values):
    high = values.astype(BF16)
    rest = values - high.astype(F32)
    middle = rest.astype(BF16)
    low = (rest - middle.astype(F32)).astype(BF16)
    copy = iota(values.shape, values.ndim - 1) & (COPIES - 1)
    parts = jnp.where(copy == 0, high.astype(F32), jnp.where(copy == 1, middle.astype(F32), low.astype(F32)))
    return jnp.where(copy < 3, parts, 0.0).astype(BF16)


def normalize(tokens):
    centre = jnp.mean(tokens, axis=-1, keepdims=True)
    moved = tokens - centre
    spread = jnp.mean(jnp.square(moved), axis=-1, keepdims=True)
    return (moved * lax.rsqrt(spread + 1e-05)).astype(BF16)


def gelu(x):
    return 0.5 * x * (1.0 + lax.erf(x * 0.7071067811865476))


def kernel(
    sizes,
    x_ref, pw_ref, ce_ref, qk_ref, vw_ref, ow_ref, de_ref, dw_ref,
    out_ref,
    state, patches, wp, wv, wo, wd, expand, keys, mixed_rows,
    pixels_in, pixels_out, rim_out, rim_in, part_out, part_in, mixed,
    tokens_a, tokens_b,
    x_sem, out_sem, w_local, w_send, w_recv, h_send, h_recv, r_send, r_recv, p_send, p_recv, m_send, m_recv,
):
    chans, cols, nchan, nband, nrep = sizes
    tokens = (tokens_a, tokens_b)
    group = min(8, chans)
    groups = chans // group
    pack = min(16, chans)
    ratio = pack // group
    packs = chans // pack
    nchunks = cols // CHUNK
    owners = nchan // nchunks
    me = lax.axis_index("chan")
    rep = lax.axis_index("rep")
    place = lax.axis_index("band") * nrep + rep
    last = nband * nrep - 1
    has_up = place > 0
    has_down = place < last
    up_place = jnp.maximum(place - 1, 0)
    down_place = jnp.minimum(place + 1, last)
    up = {"band": up_place // nrep, "rep": up_place % nrep}
    down = {"band": down_place // nrep, "rep": down_place % nrep}
    my_chunk = me // owners
    my_lane = me % owners

    tiles_across = cols // 8

    def load(t):
        return pltpu.make_async_copy(
            x_ref.at[:, t * LANES : (t + 1) * LANES], pixels_in.at[t], x_sem.at[t]
        )

    for t in range(tiles_across):
        load(t).start()

    barrier = pltpu.get_barrier_semaphore()

    @pl.when(has_up)
    def _():
        pl.semaphore_signal(barrier, inc=1, device_id=up, device_id_type=MESH)

    @pl.when(has_down)
    def _():
        pl.semaphore_signal(barrier, inc=1, device_id=down, device_id_type=MESH)

    @pl.loop(1, nchan)
    def _(i):
        pl.semaphore_signal(
            barrier, inc=1, device_id={"chan": (me + i) % nchan}, device_id_type=MESH
        )

    pl.semaphore_wait(
        barrier, nchan - 1 + jnp.minimum(place, 1) + jnp.minimum(last - place, 1)
    )

    other = {"rep": 1 - rep}
    depth = D // nrep
    rows_r = PATCH // nrep
    here_r = pl.ds(pl.multiple_of(rep * rows_r, rows_r), rows_r)
    here_d = pl.ds(pl.multiple_of(rep * depth, depth), depth)
    there_r = pl.ds(pl.multiple_of((1 - rep) * rows_r, rows_r), rows_r)
    there_d = pl.ds(pl.multiple_of((1 - rep) * depth, depth), depth)
    moves = [
        (pw_ref.at[:, 0], lambda rows, _: wp.at[0, rows]),
        (pw_ref.at[:, 1], lambda rows, _: wp.at[1, rows]),
        (vw_ref, lambda _, rows: wv.at[rows]),
        (ow_ref, lambda _, rows: wo.at[rows]),
    ]

    def local_weight(n):
        source, target = moves[n]
        return pltpu.make_async_copy(source, target(here_r, here_d), w_local.at[n])

    def remote_weight(n, rows_r_, rows_d_):
        source, target = moves[n]
        return pltpu.make_async_remote_copy(
            src_ref=source, dst_ref=target(rows_r_, rows_d_),
            send_sem=w_send.at[n], recv_sem=w_recv.at[n],
            device_id=other, device_id_type=MESH,
        )

    def remote_decoder(rows):
        return pltpu.make_async_remote_copy(
            src_ref=wd.at[rows], dst_ref=wd.at[rows],
            send_sem=w_send.at[len(moves)], recv_sem=w_recv.at[len(moves)],
            device_id=other, device_id_type=MESH,
        )

    for n in range(len(moves)):
        local_weight(n).start()
        remote_weight(n, here_r, here_d).start()

    def wait_weight(n):
        local_weight(n).wait()
        remote_weight(n, here_r, here_d).wait_send()
        remote_weight(n, there_r, there_d).wait_recv()

    lane = iota((LANES, D), 0)
    feature = lax.shift_right_logical(iota((LANES, D), 1), 6)
    expand[...] = jnp.where(
        (lax.shift_right_logical(lane, 3) == feature) & ((lane & (COPIES - 1)) < 3), 1.0, 0.0
    ).astype(BF16)

    def span(g):
        return pl.ds(pl.multiple_of(g * group, group), group)

    def bundle(p):
        return pl.ds(pl.multiple_of(p * pack, pack), pack)

    def places(p):
        return pl.ds(pl.multiple_of(p * CHUNK, CHUNK), CHUNK)

    def halo_up(s, p):
        return pltpu.make_async_remote_copy(
            src_ref=patches.at[s, places(p), :, LANES : 2 * LANES],
            dst_ref=patches.at[s, places(p), :, 3 * LANES :],
            send_sem=h_send.at[s, 0, p], recv_sem=h_recv.at[s, 1, p],
            device_id=up, device_id_type=MESH,
        )

    def halo_down(s, p):
        return pltpu.make_async_remote_copy(
            src_ref=patches.at[s, places(p), :, 2 * LANES : 3 * LANES],
            dst_ref=patches.at[s, places(p), :, :LANES],
            send_sem=h_send.at[s, 1, p], recv_sem=h_recv.at[s, 0, p],
            device_id=down, device_id_type=MESH,
        )

    def rim_up(s, g):
        return pltpu.make_async_remote_copy(
            src_ref=rim_out.at[s, 0, g], dst_ref=rim_in.at[s, 1, g],
            send_sem=r_send.at[s, 0, g], recv_sem=r_recv.at[s, 1, g],
            device_id=up, device_id_type=MESH,
        )

    def rim_down(s, g):
        return pltpu.make_async_remote_copy(
            src_ref=rim_out.at[s, 1, g], dst_ref=rim_in.at[s, 0, g],
            send_sem=r_send.at[s, 1, g], recv_sem=r_recv.at[s, 0, g],
            device_id=down, device_id_type=MESH,
        )

    def fill_own(s, p):
        patches[s, pl.ds(0, cols), bundle(p), LANES : 3 * LANES] = state[:, bundle(p), :].astype(BF16)

    def send_halos(s):
        @pl.loop(0, nchunks)
        def _(i):
            chunk = (my_chunk + 1 + i) % nchunks

            @pl.when(has_up)
            def _():
                halo_up(s, chunk).start()

            @pl.when(has_down)
            def _():
                halo_down(s, chunk).start()

    def wait_halo(s, chunk):
        @pl.when(has_up)
        def _():
            halo_up(s, chunk).wait_send()
            halo_down(s, chunk).wait_recv()

        @pl.when(has_down)
        def _():
            halo_down(s, chunk).wait_send()
            halo_up(s, chunk).wait_recv()

    for t in range(tiles_across):
        load(t).wait()

    @pl.loop(0, packs)
    def _(p):
        @pl.loop(0, ratio)
        def _(i):
            g = p * ratio + i

            @pl.loop(0, 2)
            def _(half):
                first = g * (group * STRIDE) + half * 8
                fields = [
                    pltpu.roll(
                        jnp.concatenate(
                            [
                                pixels_in[t, pl.ds(first + r, group, stride=STRIDE), :]
                                for t in range(tiles_across)
                            ],
                            axis=1,
                        ),
                        RIM, 1,
                    )
                    for r in range(8)
                ]
                there = pl.ds(pl.multiple_of(half * LANES, LANES), LANES)
                for t in range(cols // 8):
                    tiles = swap_chunks([field[:, t * LANES : (t + 1) * LANES] for field in fields])
                    for j in range(8):
                        state[t * 8 + j, span(g), there] = tiles[j]

        fill_own(0, p)

    send_halos(0)

    source = iota((2 * LANES, 2 * LANES), 0)
    target = iota((2 * LANES, 2 * LANES), 1)
    moved = (
        (lax.shift_right_logical(source, 4) & 1) * LANES
        + lax.shift_right_logical(source, 5) * STRIDE
        + (source & (STRIDE - 1))
    )
    order = jnp.where(moved == target, 1.0, 0.0).astype(BF16)
    for b in range(D // (2 * LANES)):
        ordered = jnp.dot(
            dw_ref[:, b * 2 * LANES : (b + 1) * 2 * LANES], order, preferred_element_type=F32
        ).astype(BF16)
        wd[here_d, b * LANES : (b + 1) * LANES] = ordered[:, :LANES]
        wd[here_d, D // 2 + b * LANES : D // 2 + (b + 1) * LANES] = ordered[:, LANES:]
    remote_decoder(here_d).start()

    zeros = jnp.zeros((STEPS, cols, chans, LANES), BF16)

    @pl.when(jnp.logical_not(has_up))
    def _():
        patches[:, :cols, :, :LANES] = zeros

    @pl.when(jnp.logical_not(has_down))
    def _():
        patches[:, :cols, :, 3 * LANES :] = zeros

    spots = jnp.where(
        lax.shift_right_logical(iota((LANES, HEADS), 0), 3) == iota((LANES, HEADS), 1), 1.0, 0.0
    ).astype(BF16)
    keys[...] = jnp.dot(spots, qk_ref[...], preferred_element_type=F32).astype(BF16)

    for n in range(3):
        wait_weight(n)

    def part_copy(s, to, slot):
        return pltpu.make_async_remote_copy(
            src_ref=part_out.at[s, to // owners], dst_ref=part_in.at[s, slot],
            send_sem=p_send.at[s, to], recv_sem=p_recv.at[s, slot],
            device_id={"chan": to}, device_id_type=MESH,
        )

    def mixed_copy(s, chunk, slot):
        return pltpu.make_async_remote_copy(
            src_ref=mixed.at[s, my_chunk], dst_ref=mixed.at[s, slot],
            send_sem=m_send.at[s, chunk], recv_sem=m_recv.at[s, slot],
            device_id={"chan": chunk * owners + my_lane}, device_id_type=MESH,
        )

    def store(g, t):
        rows = pl.ds(pl.multiple_of(g * (group * STRIDE), group * STRIDE), group * STRIDE)
        return pltpu.make_async_copy(
            pixels_out.at[t, rows], out_ref.at[rows, t * LANES : (t + 1) * LANES], out_sem.at[g, t]
        )

    span_rows = COPIES * chans

    def embed(s, chunk, slot):
        start = pl.multiple_of(chunk * CHUNK, CHUNK)
        rows = jnp.concatenate(
            [patches[s, pl.ds(start, CHUNK)], patches[s, pl.ds(start + 1, CHUNK)]], axis=2
        ).reshape(CHUNK * chans, D)
        embedded = jnp.dot(rows, wp[...].reshape(D, D), preferred_element_type=F32)
        embedded = embedded.reshape(CHUNK, chans, D) + ce_ref[...][None]
        tokens[slot][...] = embedded.astype(BF16).reshape(CHUNK * chans, D)

    def aggregate(s, chunk, slot):
        normed = normalize(tokens[slot][...].astype(F32))
        scores = lax.dot_general(
            normed, keys[...], (((1,), (1,)), ((), ())), preferred_element_type=F32
        )
        scores = scores.reshape(CHUNK, chans, LANES)
        peak = jnp.max(scores, axis=1, keepdims=True)
        raised = jnp.exp(scores - peak).astype(BF16).astype(F32)
        part_out[s, chunk, :, D : D + LANES] = jnp.max(scores, axis=1)
        part_out[s, chunk, :, D + LANES :] = jnp.sum(raised, axis=1)
        own = (iota(raised.shape, 2) & (COPIES - 1)) == (iota(raised.shape, 0) & (COPIES - 1))
        placed = jnp.where(own, raised, 0.0).reshape(CHUNK * chans, LANES)
        highs, lows = [], []
        for k in range(CHUNK // COPIES):
            rows = slice(k * span_rows, (k + 1) * span_rows)
            total = jnp.dot(placed[rows].T.astype(BF16), normed[rows], preferred_element_type=F32)
            high = total.astype(BF16)
            highs.append(high)
            lows.append((total - high.astype(F32)).astype(BF16))
        depth_n = WIDE // HEAD_DIM * COPIES
        head = lax.shift_right_logical(iota((COPIES, WIDE), 1), 6)
        for n in range(D // WIDE):
            rows = slice(n * depth_n, (n + 1) * depth_n)
            columns = slice(n * WIDE, (n + 1) * WIDE)
            mixed_heads = jnp.dot(
                jnp.concatenate([part[rows] for part in highs + lows], axis=0),
                wv[:, columns], preferred_element_type=F32,
            )
            for k in range(CHUNK // COPIES):
                low = (CHUNK // COPIES + k) * depth_n
                both = mixed_heads[k * depth_n : (k + 1) * depth_n] + mixed_heads[low : low + depth_n]
                kept = both[:COPIES]
                for h in range(1, WIDE // HEAD_DIM):
                    kept = jnp.where(head == h, both[h * COPIES : (h + 1) * COPIES], kept)
                part_out[s, chunk, k * COPIES : (k + 1) * COPIES, columns] = kept

    def step(s):
        order = [(my_chunk + 1 + i) % nchunks for i in range(nchunks)]
        wait_halo(s, order[0])
        for i in range(nchunks + 1):
            if i < nchunks:
                if i + 1 < nchunks:
                    wait_halo(s, order[i + 1])

                @pl.when(order[i] == nchunks - 1)
                def _():
                    patches[s, cols] = patches[s, 0]

                embed(s, order[i], i % 2)
            if i > 0:
                aggregate(s, order[i - 1], (i - 1) % 2)

                @pl.loop(0, owners)
                def _(a):
                    to = order[i - 1] * owners + a

                    @pl.when(to != me)
                    def _():
                        part_copy(s, to, me).start()

        part_in[s, me] = part_out[s, my_chunk]

        @pl.when(s == 0)
        def _():
            wait_weight(3)

        @pl.loop(1, nchan)
        def _(i):
            peer = (me + i) % nchan
            part_copy(s, peer, me).wait_send()
            part_copy(s, peer, peer).wait_recv()

        peaks = part_in[s, :, :, D : D + LANES]
        factors = jnp.exp(peaks - jnp.max(peaks, axis=0)[None])
        total = jnp.sum(factors * part_in[s, :, :, D + LANES :], axis=0)
        factors = factors / total[None]
        factors = jnp.dot(
            split_parts(factors.reshape(nchan * CHUNK, LANES)), expand[...], preferred_element_type=F32
        ).reshape(nchan, CHUNK, D)
        blended = jnp.sum(factors * part_in[s, :, :, :D], axis=0).astype(BF16)
        mixed[s, my_chunk] = jnp.dot(blended, wo[...], preferred_element_type=F32).astype(BF16)

        @pl.loop(1, nchunks)
        def _(i):
            mixed_copy(s, (my_chunk + i) % nchunks, my_chunk).start()

        @pl.when(s == 0)
        def _():
            remote_decoder(here_d).wait_send()
            remote_decoder(there_d).wait_recv()

        @pl.loop(1, nchunks)
        def _(i):
            chunk = (my_chunk + i) % nchunks
            mixed_copy(s, chunk, my_chunk).wait_send()
            mixed_copy(s, chunk, chunk).wait_recv()

        @pl.loop(0, nchunks)
        def _(n):
            rows = mixed[s, n].astype(F32)
            for j in range(CHUNK):
                mixed_rows[n * CHUNK + j] = jnp.broadcast_to(rows[j : j + 1], (group, D))

        @pl.loop(0, groups + 1)
        def _(g):
            @pl.when(g < groups)
            def _():
                hidden = gelu(mixed_rows[...] + de_ref[span(g), :][None])
                hidden = hidden.reshape(cols * group, D).astype(BF16)
                pixels = jnp.dot(hidden, wd[...], preferred_element_type=F32)
                pixels = 0.25 * pixels.reshape(cols, group, D)
                right = pixels[:, :, D // 2 :]
                blocks = pixels[:, :, : D // 2] + jnp.concatenate([right[-1:], right[:-1]], axis=0)
                rim_out[s, 0, g] = blocks[:, :, :LANES].astype(BF16)
                rim_out[s, 1, g] = blocks[:, :, 3 * LANES :].astype(BF16)

                @pl.when(has_up)
                def _():
                    rim_up(s, g).start()

                @pl.when(has_down)
                def _():
                    rim_down(s, g).start()

                state[:, span(g), :] = state[:, span(g), :] + blocks[:, :, LANES : 3 * LANES]

            @pl.when(g > 0)
            def _():
                done = g - 1

                @pl.when(has_up)
                def _():
                    rim_up(s, done).wait_send()
                    rim_down(s, done).wait_recv()
                    state[:, span(done), :LANES] = (
                        state[:, span(done), :LANES] + rim_in[s, 0, done].astype(F32)
                    )

                @pl.when(has_down)
                def _():
                    rim_down(s, done).wait_send()
                    rim_up(s, done).wait_recv()
                    state[:, span(done), LANES:] = (
                        state[:, span(done), LANES:] + rim_in[s, 1, done].astype(F32)
                    )

                @pl.when((s < STEPS - 1) & (done % ratio == ratio - 1))
                def _():
                    fill_own(s + 1, done // ratio)

                @pl.when(s == STEPS - 1)
                def _():
                    @pl.loop(0, 2)
                    def _(half):
                        first = done * (group * STRIDE) + half * 8
                        there = pl.ds(pl.multiple_of(half * LANES, LANES), LANES)
                        columns = [
                            swap_chunks([state[t * 8 + j, span(done), there] for j in range(8)])
                            for t in range(cols // 8)
                        ]
                        for r in range(8):
                            field = jnp.concatenate([tiles[r] for tiles in columns], axis=1)
                            field = pltpu.roll(field, field.shape[1] - RIM, 1)
                            for t in range(tiles_across):
                                pixels_out[t, pl.ds(first + r, group, stride=STRIDE), :] = field[
                                    :, t * LANES : (t + 1) * LANES
                                ]

                    for t in range(tiles_across):
                        store(done, t).start()

    @pl.loop(0, STEPS)
    def _(s):
        step(s)

        @pl.when(s < STEPS - 1)
        def _():
            send_halos(s + 1)

    @pl.loop(0, groups)
    def _(g):
        for t in range(tiles_across):
            store(g, t).wait()


def body(mesh_sizes, state_field, patch_weight, chan_embed, query_keys, value_weight, out_weight, dec_embed, dec_weight):
    nchan, nband, nrep = mesh_sizes
    chans, rows, width = state_field.shape
    cols = width // STRIDE
    group = min(8, chans)
    groups = chans // group
    nchunks = cols // CHUNK
    assert rows == STRIDE and nrep == 2 and nchan % nchunks == 0
    vmem = pl.BlockSpec(memory_space=pltpu.VMEM)
    whole = pl.BlockSpec(memory_space=pl.ANY)
    dma = pltpu.SemaphoreType.DMA
    return pl.pallas_call(
        functools.partial(kernel, (chans, cols, nchan, nband, nrep)),
        out_shape=jax.ShapeDtypeStruct((chans * rows, width), F32),
        in_specs=[whole, whole, vmem, vmem, whole, whole, vmem, vmem],
        out_specs=whole,
        scratch_shapes=[
            pltpu.VMEM((cols, chans, 2 * LANES), F32),
            pltpu.VMEM((STEPS, cols + 1, chans, D // 2), BF16),
            pltpu.VMEM((2, PATCH, STRIDE, D), BF16),
            pltpu.VMEM((D, D), BF16),
            pltpu.VMEM((D, D), BF16),
            pltpu.VMEM((D, D), BF16),
            pltpu.VMEM((LANES, D), BF16),
            pltpu.VMEM((LANES, D), BF16),
            pltpu.VMEM((cols, group, D), F32),
            pltpu.VMEM((cols // 8, chans * rows, LANES), F32),
            pltpu.VMEM((cols // 8, chans * rows, LANES), F32),
            pltpu.VMEM((STEPS, 2, groups, cols, group, LANES), BF16),
            pltpu.VMEM((STEPS, 2, groups, cols, group, LANES), BF16),
            pltpu.VMEM((STEPS, nchunks, CHUNK, PACKET), F32),
            pltpu.VMEM((STEPS, nchan, CHUNK, PACKET), F32),
            pltpu.VMEM((STEPS, nchunks, CHUNK, D), BF16),
            pltpu.VMEM((CHUNK * chans, D), BF16),
            pltpu.VMEM((CHUNK * chans, D), BF16),
            dma((cols // 8,)), dma((groups, cols // 8)), dma((4,)), dma((5,)), dma((5,)),
            dma((STEPS, 2, nchunks)), dma((STEPS, 2, nchunks)),
            dma((STEPS, 2, groups)), dma((STEPS, 2, groups)),
            dma((STEPS, nchan)), dma((STEPS, nchan)),
            dma((STEPS, nchunks)), dma((STEPS, nchunks)),
        ],
        compiler_params=pltpu.CompilerParams(
            collective_id=0, has_side_effects=True, vmem_limit_bytes=60 * 1024 * 1024
        ),
        name="rollout",
    )(
        state_field.reshape(chans * rows, width),
        patch_weight.reshape(PATCH // nrep, 2, STRIDE, D),
        chan_embed,
        query_keys.T,
        value_weight,
        out_weight,
        dec_embed,
        dec_weight,
    ).reshape(state_field.shape)


def solution(mesh):
    in_specs = (
        P(("groups", "chan"), ("band", "rep"), None),
        P("rep", None),
        P("chan", None),
        P(),
        P("rep", None),
        P("rep", None),
        P("chan", None),
        P("rep", None),
    )
    out_specs = P(("groups", "chan"), ("band", "rep"), None)
    sizes = (mesh.shape["chan"], mesh.shape["band"], mesh.shape["rep"])
    return jax.shard_map(
        functools.partial(body, sizes), mesh=mesh, in_specs=in_specs, out_specs=out_specs, check_vma=False
    )
```

```python
import functools

import jax
import jax.numpy as jnp
from jax import lax
from jax.experimental import pallas as pl
from jax.experimental.pallas import tpu as pltpu
from jax.sharding import PartitionSpec as P

D = 1024
HEADS = 16
HEAD_DIM = D // HEADS
PATCH = 32
STRIDE = 16
RIM = 8
STEPS = 2
LANES = 128
COPIES = LANES // HEADS
CHUNK = 16
WIDE = 256
LAG = 2
PACKET = D + 2 * LANES
MESH = pl.DeviceIdType.MESH
F32 = jnp.float32
BF16 = jnp.bfloat16


def iota(shape, dim):
    return lax.broadcasted_iota(jnp.int32, shape, dim)


def swap_chunks(tiles):
    tiles = list(tiles)
    chunk = lax.shift_right_logical(iota(tiles[0].shape, 1), 4)
    for bit in (1, 2, 4):
        high = (chunk & bit) != 0
        for low in range(8):
            if low & bit:
                continue
            first, second = tiles[low], tiles[low + bit]
            tiles[low] = jnp.where(high, pltpu.roll(second, 16 * bit, 1), first)
            tiles[low + bit] = jnp.where(high, second, pltpu.roll(first, LANES - 16 * bit, 1))
    return tiles


def split_parts(values):
    high = values.astype(BF16)
    rest = values - high.astype(F32)
    middle = rest.astype(BF16)
    low = (rest - middle.astype(F32)).astype(BF16)
    copy = iota(values.shape, values.ndim - 1) & (COPIES - 1)
    parts = jnp.where(copy == 0, high.astype(F32), jnp.where(copy == 1, middle.astype(F32), low.astype(F32)))
    return jnp.where(copy < 3, parts, 0.0).astype(BF16)


def normalize(tokens):
    centre = jnp.mean(tokens, axis=-1, keepdims=True)
    moved = tokens - centre
    spread = jnp.mean(jnp.square(moved), axis=-1, keepdims=True)
    return (moved * lax.rsqrt(spread + 1e-05)).astype(BF16)


def gelu(x):
    return 0.5 * x * (1.0 + lax.erf(x * 0.7071067811865476))


def kernel(
    sizes,
    x_ref, pw_ref, ce_ref, qk_ref, vw_ref, ow_ref, de_ref, dw_ref,
    out_ref,
    state, patches, wp, wv, wo, wd, expand, keys, mixed_rows,
    pixels_in, rim_out, rim_in, edge_out, edge_in, carry, part_out, part_in, mixed,
    tokens_a, tokens_b,
    x_sem, out_sem, w_local, w_send, w_recv, h_send, h_recv, r_send, r_recv, p_send, p_recv, m_send, m_recv,
):
    chans, cols, nchan, nband, nrep = sizes
    tokens = (tokens_a, tokens_b)
    group = min(8, chans)
    groups = chans // group
    pack = min(16, chans)
    ratio = pack // group
    packs = chans // pack
    nchunks = cols // CHUNK
    owners = nchan // nchunks
    me = lax.axis_index("chan")
    rep = lax.axis_index("rep")
    place = lax.axis_index("band") * nrep + rep
    last = nband * nrep - 1
    has_up = place > 0
    has_down = place < last
    up_place = jnp.maximum(place - 1, 0)
    down_place = jnp.minimum(place + 1, last)
    up = {"band": up_place // nrep, "rep": up_place % nrep}
    down = {"band": down_place // nrep, "rep": down_place % nrep}
    my_chunk = me // owners
    my_lane = me % owners

    tiles_across = cols // 8

    def load(t):
        return pltpu.make_async_copy(
            x_ref.at[:, t * LANES : (t + 1) * LANES], pixels_in.at[t], x_sem.at[t]
        )

    for t in range(tiles_across):
        load(t).start()

    barrier = pltpu.get_barrier_semaphore()

    @pl.when(has_up)
    def _():
        pl.semaphore_signal(barrier, inc=1, device_id=up, device_id_type=MESH)

    @pl.when(has_down)
    def _():
        pl.semaphore_signal(barrier, inc=1, device_id=down, device_id_type=MESH)

    @pl.loop(1, nchan)
    def _(i):
        pl.semaphore_signal(
            barrier, inc=1, device_id={"chan": (me + i) % nchan}, device_id_type=MESH
        )

    pl.semaphore_wait(
        barrier, nchan - 1 + jnp.minimum(place, 1) + jnp.minimum(last - place, 1)
    )

    other = {"rep": 1 - rep}
    depth = D // nrep
    rows_r = PATCH // nrep
    here_r = pl.ds(pl.multiple_of(rep * rows_r, rows_r), rows_r)
    here_d = pl.ds(pl.multiple_of(rep * depth, depth), depth)
    there_r = pl.ds(pl.multiple_of((1 - rep) * rows_r, rows_r), rows_r)
    there_d = pl.ds(pl.multiple_of((1 - rep) * depth, depth), depth)
    moves = [
        (pw_ref.at[:, 0], lambda rows, _: wp.at[0, rows]),
        (pw_ref.at[:, 1], lambda rows, _: wp.at[1, rows]),
        (vw_ref, lambda _, rows: wv.at[rows]),
        (ow_ref, lambda _, rows: wo.at[rows]),
    ]

    def local_weight(n):
        source, target = moves[n]
        return pltpu.make_async_copy(source, target(here_r, here_d), w_local.at[n])

    def remote_weight(n, rows_r_, rows_d_):
        source, target = moves[n]
        return pltpu.make_async_remote_copy(
            src_ref=source, dst_ref=target(rows_r_, rows_d_),
            send_sem=w_send.at[n], recv_sem=w_recv.at[n],
            device_id=other, device_id_type=MESH,
        )

    def remote_decoder(rows):
        return pltpu.make_async_remote_copy(
            src_ref=wd.at[rows], dst_ref=wd.at[rows],
            send_sem=w_send.at[len(moves)], recv_sem=w_recv.at[len(moves)],
            device_id=other, device_id_type=MESH,
        )

    for n in range(len(moves)):
        local_weight(n).start()
        remote_weight(n, here_r, here_d).start()

    def wait_weight(n):
        local_weight(n).wait()
        remote_weight(n, here_r, here_d).wait_send()
        remote_weight(n, there_r, there_d).wait_recv()

    lane = iota((LANES, D), 0)
    feature = lax.shift_right_logical(iota((LANES, D), 1), 6)
    expand[...] = jnp.where(
        (lax.shift_right_logical(lane, 3) == feature) & ((lane & (COPIES - 1)) < 3), 1.0, 0.0
    ).astype(BF16)

    def span(g):
        return pl.ds(pl.multiple_of(g * group, group), group)

    def bundle(p):
        return pl.ds(pl.multiple_of(p * pack, pack), pack)

    def places(p):
        return pl.ds(pl.multiple_of(p * CHUNK, CHUNK), CHUNK)

    def halo_up(s, n, first, count):
        return pltpu.make_async_remote_copy(
            src_ref=patches.at[s, pl.ds(first, count), :, LANES : 2 * LANES],
            dst_ref=patches.at[s, pl.ds(first, count), :, 3 * LANES :],
            send_sem=h_send.at[s, 0, n], recv_sem=h_recv.at[s, 1, n],
            device_id=up, device_id_type=MESH,
        )

    def halo_down(s, n, first, count):
        return pltpu.make_async_remote_copy(
            src_ref=patches.at[s, pl.ds(first, count), :, 2 * LANES : 3 * LANES],
            dst_ref=patches.at[s, pl.ds(first, count), :, :LANES],
            send_sem=h_send.at[s, 1, n], recv_sem=h_recv.at[s, 0, n],
            device_id=down, device_id_type=MESH,
        )

    def rim_up(s, n):
        return pltpu.make_async_remote_copy(
            src_ref=rim_out.at[s, 0, n], dst_ref=rim_in.at[s, 1, n],
            send_sem=r_send.at[s, 0, n], recv_sem=r_recv.at[s, 1, n],
            device_id=up, device_id_type=MESH,
        )

    def rim_down(s, n):
        return pltpu.make_async_remote_copy(
            src_ref=rim_out.at[s, 1, n], dst_ref=rim_in.at[s, 0, n],
            send_sem=r_send.at[s, 1, n], recv_sem=r_recv.at[s, 0, n],
            device_id=down, device_id_type=MESH,
        )

    def edge_up(s):
        return pltpu.make_async_remote_copy(
            src_ref=edge_out.at[s, 0], dst_ref=edge_in.at[s, 1],
            send_sem=r_send.at[s, 0, nchunks], recv_sem=r_recv.at[s, 1, nchunks],
            device_id=up, device_id_type=MESH,
        )

    def edge_down(s):
        return pltpu.make_async_remote_copy(
            src_ref=edge_out.at[s, 1], dst_ref=edge_in.at[s, 0],
            send_sem=r_send.at[s, 1, nchunks], recv_sem=r_recv.at[s, 0, nchunks],
            device_id=down, device_id_type=MESH,
        )

    seam = my_chunk * CHUNK

    def fill_own(s, p):
        patches[s, pl.ds(0, cols), bundle(p), LANES : 3 * LANES] = state[:, bundle(p), :].astype(BF16)

    def send_halo(s, n, first, count):
        @pl.when(has_up)
        def _():
            halo_up(s, n, first, count).start()

        @pl.when(has_down)
        def _():
            halo_down(s, n, first, count).start()

    def wait_halo(s, n, first, count):
        @pl.when(has_up)
        def _():
            halo_up(s, n, first, count).wait_send()
            halo_down(s, n, first, count).wait_recv()

        @pl.when(has_down)
        def _():
            halo_down(s, n, first, count).wait_send()
            halo_up(s, n, first, count).wait_recv()

    for t in range(tiles_across):
        load(t).wait()

    @pl.loop(0, packs)
    def _(p):
        @pl.loop(0, ratio)
        def _(i):
            g = p * ratio + i

            @pl.loop(0, 2)
            def _(half):
                first = g * (group * STRIDE) + half * 8
                fields = [
                    pltpu.roll(
                        jnp.concatenate(
                            [
                                pixels_in[t, pl.ds(first + r, group, stride=STRIDE), :]
                                for t in range(tiles_across)
                            ],
                            axis=1,
                        ),
                        RIM, 1,
                    )
                    for r in range(8)
                ]
                there = pl.ds(pl.multiple_of(half * LANES, LANES), LANES)
                for t in range(cols // 8):
                    tiles = swap_chunks([field[:, t * LANES : (t + 1) * LANES] for field in fields])
                    for j in range(8):
                        state[t * 8 + j, span(g), there] = tiles[j]

        fill_own(0, p)

    for i in range(1, nchunks):
        chunk = (my_chunk + i) % nchunks
        send_halo(0, chunk, chunk * CHUNK, CHUNK)
    send_halo(0, nchunks, seam, 1)
    send_halo(0, my_chunk, seam + 1, CHUNK - 1)

    source = iota((2 * LANES, 2 * LANES), 0)
    target = iota((2 * LANES, 2 * LANES), 1)
    moved = (
        (lax.shift_right_logical(source, 4) & 1) * LANES
        + lax.shift_right_logical(source, 5) * STRIDE
        + (source & (STRIDE - 1))
    )
    order = jnp.where(moved == target, 1.0, 0.0).astype(BF16)
    for b in range(D // (2 * LANES)):
        ordered = jnp.dot(
            dw_ref[:, b * 2 * LANES : (b + 1) * 2 * LANES], order, preferred_element_type=F32
        )
        ordered = (0.25 * ordered).astype(BF16)
        wd[here_d, b * LANES : (b + 1) * LANES] = ordered[:, :LANES]
        wd[here_d, D // 2 + b * LANES : D // 2 + (b + 1) * LANES] = ordered[:, LANES:]
    remote_decoder(here_d).start()

    zeros = jnp.zeros((STEPS, cols, chans, LANES), BF16)

    @pl.when(jnp.logical_not(has_up))
    def _():
        patches[:, :cols, :, :LANES] = zeros

    @pl.when(jnp.logical_not(has_down))
    def _():
        patches[:, :cols, :, 3 * LANES :] = zeros

    spots = jnp.where(
        lax.shift_right_logical(iota((LANES, HEADS), 0), 3) == iota((LANES, HEADS), 1), 1.0, 0.0
    ).astype(BF16)
    keys[...] = jnp.dot(spots, qk_ref[...], preferred_element_type=F32).astype(BF16)

    for n in range(3):
        wait_weight(n)

    def part_copy(s, to, slot):
        return pltpu.make_async_remote_copy(
            src_ref=part_out.at[s, to // owners], dst_ref=part_in.at[s, slot],
            send_sem=p_send.at[s, to], recv_sem=p_recv.at[s, slot],
            device_id={"chan": to}, device_id_type=MESH,
        )

    def mixed_copy(s, chunk, slot):
        return pltpu.make_async_remote_copy(
            src_ref=mixed.at[s, my_chunk], dst_ref=mixed.at[s, slot],
            send_sem=m_send.at[s, chunk], recv_sem=m_recv.at[s, slot],
            device_id={"chan": chunk * owners + my_lane}, device_id_type=MESH,
        )

    def store(n, first, count):
        return pltpu.make_async_copy(
            state.at[pl.ds(first, count)], out_ref.at[pl.ds(first, count)], out_sem.at[n]
        )

    span_rows = COPIES * chans

    def embed(s, chunk, slot):
        start = pl.multiple_of(chunk * CHUNK, CHUNK)
        rows = jnp.concatenate(
            [patches[s, pl.ds(start, CHUNK)], patches[s, pl.ds(start + 1, CHUNK)]], axis=2
        ).reshape(CHUNK * chans, D)
        embedded = jnp.dot(rows, wp[...].reshape(D, D), preferred_element_type=F32)
        embedded = embedded.reshape(CHUNK, chans, D) + ce_ref[...][None]
        tokens[slot][...] = embedded.astype(BF16).reshape(CHUNK * chans, D)

    def aggregate(s, chunk, slot):
        normed = normalize(tokens[slot][...].astype(F32))
        scores = lax.dot_general(
            normed, keys[...], (((1,), (1,)), ((), ())), preferred_element_type=F32
        )
        scores = scores.reshape(CHUNK, chans, LANES)
        peak = jnp.max(scores, axis=1, keepdims=True)
        raised = jnp.exp(scores - peak).astype(BF16).astype(F32)
        part_out[s, chunk, :, D : D + LANES] = jnp.max(scores, axis=1)
        part_out[s, chunk, :, D + LANES :] = jnp.sum(raised, axis=1)
        own = (iota(raised.shape, 2) & (COPIES - 1)) == (iota(raised.shape, 0) & (COPIES - 1))
        placed = jnp.where(own, raised, 0.0).reshape(CHUNK * chans, LANES)
        highs, lows = [], []
        for k in range(CHUNK // COPIES):
            rows = slice(k * span_rows, (k + 1) * span_rows)
            total = jnp.dot(placed[rows].T.astype(BF16), normed[rows], preferred_element_type=F32)
            high = total.astype(BF16)
            highs.append(high)
            lows.append((total - high.astype(F32)).astype(BF16))
        depth_n = WIDE // HEAD_DIM * COPIES
        head = lax.shift_right_logical(iota((COPIES, WIDE), 1), 6)
        for n in range(D // WIDE):
            rows = slice(n * depth_n, (n + 1) * depth_n)
            columns = slice(n * WIDE, (n + 1) * WIDE)
            mixed_heads = jnp.dot(
                jnp.concatenate([part[rows] for part in highs + lows], axis=0),
                wv[:, columns], preferred_element_type=F32,
            )
            for k in range(CHUNK // COPIES):
                low = (CHUNK // COPIES + k) * depth_n
                both = mixed_heads[k * depth_n : (k + 1) * depth_n] + mixed_heads[low : low + depth_n]
                kept = both[:COPIES]
                for h in range(1, WIDE // HEAD_DIM):
                    kept = jnp.where(head == h, both[h * COPIES : (h + 1) * COPIES], kept)
                part_out[s, chunk, k * COPIES : (k + 1) * COPIES, columns] = kept

    def step(s):
        order = [(my_chunk + 1 + i) % nchunks for i in range(nchunks)]
        wait_halo(s, order[0], order[0] * CHUNK, CHUNK)
        for i in range(nchunks + 1):
            if i < nchunks:
                if i + 2 < nchunks:
                    wait_halo(s, order[i + 1], order[i + 1] * CHUNK, CHUNK)
                elif i + 2 == nchunks:
                    wait_halo(s, nchunks, seam, 1)
                else:
                    wait_halo(s, my_chunk, seam + 1, CHUNK - 1)

                @pl.when(order[i] == nchunks - 1)
                def _():
                    patches[s, cols] = patches[s, 0]

                embed(s, order[i], i % 2)
            if i > 0:
                aggregate(s, order[i - 1], (i - 1) % 2)

                @pl.loop(0, owners)
                def _(a):
                    to = order[i - 1] * owners + a

                    @pl.when(to != me)
                    def _():
                        part_copy(s, to, me).start()

        part_in[s, me] = part_out[s, my_chunk]

        @pl.when(s == 0)
        def _():
            wait_weight(3)

        @pl.loop(1, nchan)
        def _(i):
            peer = (me + i) % nchan
            part_copy(s, peer, me).wait_send()
            part_copy(s, peer, peer).wait_recv()

        peaks = part_in[s, :, :, D : D + LANES]
        factors = jnp.exp(peaks - jnp.max(peaks, axis=0)[None])
        total = jnp.sum(factors * part_in[s, :, :, D + LANES :], axis=0)
        factors = factors / total[None]
        factors = jnp.dot(
            split_parts(factors.reshape(nchan * CHUNK, LANES)), expand[...], preferred_element_type=F32
        ).reshape(nchan, CHUNK, D)
        blended = jnp.sum(factors * part_in[s, :, :, :D], axis=0).astype(BF16)
        mixed[s, my_chunk] = jnp.dot(blended, wo[...], preferred_element_type=F32).astype(BF16)

        @pl.loop(1, nchunks)
        def _(i):
            mixed_copy(s, (my_chunk + i) % nchunks, my_chunk).start()

        @pl.when(s == 0)
        def _():
            remote_decoder(here_d).wait_send()
            remote_decoder(there_d).wait_recv()

        carry[...] = jnp.zeros_like(carry)

        @pl.loop(0, nchunks + LAG)
        def _(i):
            @pl.when(i < nchunks)
            def _():
                chunk = (my_chunk + i) % nchunks

                @pl.when(i > 0)
                def _():
                    mixed_copy(s, chunk, my_chunk).wait_send()
                    mixed_copy(s, chunk, chunk).wait_recv()

                rows = mixed[s, chunk].astype(F32)
                for j in range(CHUNK):
                    mixed_rows[j] = jnp.broadcast_to(rows[j : j + 1], (group, D))
                hidden = gelu(
                    mixed_rows[...][:, None] + de_ref[...].reshape(groups, group, D)[None]
                ).reshape(CHUNK * chans, D).astype(BF16)
                pixels = jnp.dot(hidden, wd[...], preferred_element_type=F32).reshape(CHUNK, chans, D)
                right = pixels[:, :, D // 2 :]
                blocks = pixels[:, :, : D // 2] + jnp.concatenate([carry[...][None], right[:-1]], axis=0)
                carry[...] = right[CHUNK - 1]
                rim_out[s, 0, chunk] = blocks[:, :, :LANES].astype(BF16)
                rim_out[s, 1, chunk] = blocks[:, :, 3 * LANES :].astype(BF16)

                @pl.when(has_up)
                def _():
                    rim_up(s, chunk).start()

                @pl.when(has_down)
                def _():
                    rim_down(s, chunk).start()

                state[places(chunk)] = state[places(chunk)] + blocks[:, :, LANES : 3 * LANES]

                @pl.when(i == nchunks - 1)
                def _():
                    edge_out[s, 0] = carry[:, :LANES].astype(BF16)
                    edge_out[s, 1] = carry[:, 3 * LANES :].astype(BF16)

                    @pl.when(has_up)
                    def _():
                        edge_up(s).start()

                    @pl.when(has_down)
                    def _():
                        edge_down(s).start()

                    state[seam] = state[seam] + carry[:, LANES : 3 * LANES]

            @pl.when(i >= LAG)
            def _():
                chunk = (my_chunk + i - LAG) % nchunks

                @pl.when(has_up)
                def _():
                    rim_up(s, chunk).wait_send()
                    rim_down(s, chunk).wait_recv()
                    state[places(chunk), :, :LANES] = (
                        state[places(chunk), :, :LANES] + rim_in[s, 0, chunk].astype(F32)
                    )

                @pl.when(has_down)
                def _():
                    rim_down(s, chunk).wait_send()
                    rim_up(s, chunk).wait_recv()
                    state[places(chunk), :, LANES:] = (
                        state[places(chunk), :, LANES:] + rim_in[s, 1, chunk].astype(F32)
                    )

                @pl.when(s < STEPS - 1)
                def _():
                    patches[s + 1, places(chunk), :, LANES : 3 * LANES] = state[places(chunk)].astype(BF16)

                    @pl.when(i == LAG)
                    def _():
                        send_halo(s + 1, my_chunk, seam + 1, CHUNK - 1)

                    @pl.when(i > LAG)
                    def _():
                        send_halo(s + 1, chunk, chunk * CHUNK, CHUNK)

                @pl.when(s == STEPS - 1)
                def _():
                    @pl.when(i == LAG)
                    def _():
                        store(my_chunk, seam + 1, CHUNK - 1).start()

                    @pl.when(i > LAG)
                    def _():
                        store(chunk, chunk * CHUNK, CHUNK).start()

        @pl.when(has_up)
        def _():
            edge_up(s).wait_send()
            edge_down(s).wait_recv()
            state[seam, :, :LANES] = state[seam, :, :LANES] + edge_in[s, 0].astype(F32)

        @pl.when(has_down)
        def _():
            edge_down(s).wait_send()
            edge_up(s).wait_recv()
            state[seam, :, LANES:] = state[seam, :, LANES:] + edge_in[s, 1].astype(F32)

        @pl.when(s < STEPS - 1)
        def _():
            patches[s + 1, seam, :, LANES : 3 * LANES] = state[seam].astype(BF16)
            send_halo(s + 1, nchunks, seam, 1)

    @pl.loop(0, STEPS)
    def _(s):
        step(s)

    store(nchunks, seam, 1).start()
    store(my_chunk, seam + 1, CHUNK - 1).wait()
    for i in range(1, nchunks):
        chunk = (my_chunk + i) % nchunks
        store(chunk, chunk * CHUNK, CHUNK).wait()
    store(nchunks, seam, 1).wait()


def lay_kernel(chans, cols, blocks_ref, out_ref, held, pixels_out, in_sem, out_sem):
    group = min(8, chans)
    groups = chans // group
    tiles_across = cols // 8

    def load(g):
        return pltpu.make_async_copy(
            blocks_ref.at[:, pl.ds(pl.multiple_of(g * group, group), group)], held.at[g], in_sem.at[g]
        )

    def store(g, t):
        rows = pl.ds(pl.multiple_of(g * (group * STRIDE), group * STRIDE), group * STRIDE)
        return pltpu.make_async_copy(
            pixels_out.at[t, rows], out_ref.at[rows, t * LANES : (t + 1) * LANES], out_sem.at[g, t]
        )

    for g in range(groups):
        load(g).start()

    @pl.loop(0, groups)
    def _(g):
        load(g).wait()

        @pl.loop(0, 2)
        def _(half):
            first = g * (group * STRIDE) + half * 8
            there = pl.ds(pl.multiple_of(half * LANES, LANES), LANES)
            columns = [
                swap_chunks([held[g, t * 8 + j, :, there] for j in range(8)]) for t in range(cols // 8)
            ]
            for r in range(8):
                field = jnp.concatenate([tiles[r] for tiles in columns], axis=1)
                field = pltpu.roll(field, field.shape[1] - RIM, 1)
                for t in range(tiles_across):
                    pixels_out[t, pl.ds(first + r, group, stride=STRIDE), :] = field[
                        :, t * LANES : (t + 1) * LANES
                    ]

        for t in range(tiles_across):
            store(g, t).start()

    @pl.loop(0, groups)
    def _(g):
        for t in range(tiles_across):
            store(g, t).wait()


def body(mesh_sizes, state_field, patch_weight, chan_embed, query_keys, value_weight, out_weight, dec_embed, dec_weight):
    nchan, nband, nrep = mesh_sizes
    chans, rows, width = state_field.shape
    cols = width // STRIDE
    group = min(8, chans)
    groups = chans // group
    nchunks = cols // CHUNK
    assert rows == STRIDE and nrep == 2 and nchan % nchunks == 0
    vmem = pl.BlockSpec(memory_space=pltpu.VMEM)
    whole = pl.BlockSpec(memory_space=pl.ANY)
    dma = pltpu.SemaphoreType.DMA
    blocks = pl.pallas_call(
        functools.partial(kernel, (chans, cols, nchan, nband, nrep)),
        out_shape=jax.ShapeDtypeStruct((cols, chans, 2 * LANES), F32),
        in_specs=[whole, whole, vmem, vmem, whole, whole, vmem, vmem],
        out_specs=whole,
        scratch_shapes=[
            pltpu.VMEM((cols, chans, 2 * LANES), F32),
            pltpu.VMEM((STEPS, cols + 1, chans, D // 2), BF16),
            pltpu.VMEM((2, PATCH, STRIDE, D), BF16),
            pltpu.VMEM((D, D), BF16),
            pltpu.VMEM((D, D), BF16),
            pltpu.VMEM((D, D), BF16),
            pltpu.VMEM((LANES, D), BF16),
            pltpu.VMEM((LANES, D), BF16),
            pltpu.VMEM((CHUNK, group, D), F32),
            pltpu.VMEM((cols // 8, chans * rows, LANES), F32),
            pltpu.VMEM((STEPS, 2, nchunks, CHUNK, chans, LANES), BF16),
            pltpu.VMEM((STEPS, 2, nchunks, CHUNK, chans, LANES), BF16),
            pltpu.VMEM((STEPS, 2, chans, LANES), BF16),
            pltpu.VMEM((STEPS, 2, chans, LANES), BF16),
            pltpu.VMEM((chans, D // 2), F32),
            pltpu.VMEM((STEPS, nchunks, CHUNK, PACKET), F32),
            pltpu.VMEM((STEPS, nchan, CHUNK, PACKET), F32),
            pltpu.VMEM((STEPS, nchunks, CHUNK, D), BF16),
            pltpu.VMEM((CHUNK * chans, D), BF16),
            pltpu.VMEM((CHUNK * chans, D), BF16),
            dma((cols // 8,)), dma((nchunks + 1,)), dma((4,)), dma((5,)), dma((5,)),
            dma((STEPS, 2, nchunks + 1)), dma((STEPS, 2, nchunks + 1)),
            dma((STEPS, 2, nchunks + 1)), dma((STEPS, 2, nchunks + 1)),
            dma((STEPS, nchan)), dma((STEPS, nchan)),
            dma((STEPS, nchunks)), dma((STEPS, nchunks)),
        ],
        compiler_params=pltpu.CompilerParams(
            collective_id=0, has_side_effects=True, vmem_limit_bytes=60 * 1024 * 1024
        ),
        name="rollout",
    )(
        state_field.reshape(chans * rows, width),
        patch_weight.reshape(PATCH // nrep, 2, STRIDE, D),
        chan_embed,
        query_keys.T,
        value_weight,
        out_weight,
        dec_embed,
        dec_weight,
    )
    return pl.pallas_call(
        functools.partial(lay_kernel, chans, cols),
        out_shape=jax.ShapeDtypeStruct((chans * rows, width), F32),
        in_specs=[whole],
        out_specs=whole,
        scratch_shapes=[
            pltpu.VMEM((groups, cols, group, 2 * LANES), F32),
            pltpu.VMEM((cols // 8, chans * rows, LANES), F32),
            dma((groups,)), dma((groups, cols // 8)),
        ],
        compiler_params=pltpu.CompilerParams(vmem_limit_bytes=16 * 1024 * 1024),
        name="lay",
    )(blocks).reshape(state_field.shape)


def solution(mesh):
    in_specs = (
        P(("groups", "chan"), ("band", "rep"), None),
        P("rep", None),
        P("chan", None),
        P(),
        P("rep", None),
        P("rep", None),
        P("chan", None),
        P("rep", None),
    )
    out_specs = P(("groups", "chan"), ("band", "rep"), None)
    sizes = (mesh.shape["chan"], mesh.shape["band"], mesh.shape["rep"])
    return jax.shard_map(
        functools.partial(body, sizes), mesh=mesh, in_specs=in_specs, out_specs=out_specs, check_vma=False
    )
```

```python
import functools

import jax
import jax.numpy as jnp
from jax import lax
from jax.experimental import pallas as pl
from jax.experimental.pallas import tpu as pltpu
from jax.sharding import PartitionSpec as P

D = 1024
HEADS = 16
HEAD_DIM = D // HEADS
PATCH = 32
STRIDE = 16
RIM = 8
STEPS = 2
LANES = 128
COPIES = LANES // HEADS
CHUNK = 16
WIDE = 256
LAG = 2
PACKET = D + 2 * LANES
MESH = pl.DeviceIdType.MESH
F32 = jnp.float32
BF16 = jnp.bfloat16


def iota(shape, dim):
    return lax.broadcasted_iota(jnp.int32, shape, dim)


def swap_chunks(tiles):
    tiles = list(tiles)
    chunk = lax.shift_right_logical(iota(tiles[0].shape, 1), 4)
    for bit in (1, 2, 4):
        high = (chunk & bit) != 0
        for low in range(8):
            if low & bit:
                continue
            first, second = tiles[low], tiles[low + bit]
            if bit == 4:
                moved = pltpu.roll(jnp.where(high, first, second), LANES // 2, 1)
                tiles[low] = jnp.where(high, moved, first)
                tiles[low + bit] = jnp.where(high, second, moved)
                continue
            tiles[low] = jnp.where(high, pltpu.roll(second, 16 * bit, 1), first)
            tiles[low + bit] = jnp.where(high, second, pltpu.roll(first, LANES - 16 * bit, 1))
    return tiles


def split_parts(values):
    high = values.astype(BF16)
    rest = values - high.astype(F32)
    middle = rest.astype(BF16)
    low = (rest - middle.astype(F32)).astype(BF16)
    copy = iota(values.shape, values.ndim - 1) & (COPIES - 1)
    parts = jnp.where(copy == 0, high.astype(F32), jnp.where(copy == 1, middle.astype(F32), low.astype(F32)))
    return jnp.where(copy < 3, parts, 0.0).astype(BF16)


def normalize(tokens):
    centre = jnp.mean(tokens, axis=-1, keepdims=True)
    moved = tokens - centre
    spread = jnp.mean(jnp.square(moved), axis=-1, keepdims=True)
    return (moved * lax.rsqrt(spread + 1e-05)).astype(BF16)


def gelu(x):
    return 0.5 * x * (1.0 + lax.erf(x * 0.7071067811865476))


def kernel(
    sizes,
    x_ref, pw_ref, ce_ref, qk_ref, vw_ref, ow_ref, de_ref, dw_ref,
    out_ref,
    state, patches, wp, wv, wo, wd, expand, keys, mixed_rows,
    pixels_in, rim_out, rim_in, edge_out, edge_in, carry, part_out, part_in, mixed,
    tokens_a, tokens_b, normed,
    x_sem, out_sem, w_local, w_send, w_recv, h_send, h_recv, r_send, r_recv, p_send, p_recv, m_send, m_recv,
):
    chans, cols, nchan, nband, nrep = sizes
    tokens = (tokens_a, tokens_b)
    group = min(8, chans)
    groups = chans // group
    pack = min(16, chans)
    ratio = pack // group
    packs = chans // pack
    nchunks = cols // CHUNK
    owners = nchan // nchunks
    me = lax.axis_index("chan")
    rep = lax.axis_index("rep")
    place = lax.axis_index("band") * nrep + rep
    last = nband * nrep - 1
    has_up = place > 0
    has_down = place < last
    up_place = jnp.maximum(place - 1, 0)
    down_place = jnp.minimum(place + 1, last)
    up = {"band": up_place // nrep, "rep": up_place % nrep}
    down = {"band": down_place // nrep, "rep": down_place % nrep}
    my_chunk = me // owners
    my_lane = me % owners

    tiles_across = cols // 8

    def load(t):
        return pltpu.make_async_copy(
            x_ref.at[:, t * LANES : (t + 1) * LANES], pixels_in.at[t], x_sem.at[t]
        )

    for t in range(tiles_across):
        load(t).start()

    barrier = pltpu.get_barrier_semaphore()

    @pl.when(has_up)
    def _():
        pl.semaphore_signal(barrier, inc=1, device_id=up, device_id_type=MESH)

    @pl.when(has_down)
    def _():
        pl.semaphore_signal(barrier, inc=1, device_id=down, device_id_type=MESH)

    @pl.loop(1, nchan)
    def _(i):
        pl.semaphore_signal(
            barrier, inc=1, device_id={"chan": (me + i) % nchan}, device_id_type=MESH
        )

    pl.semaphore_wait(
        barrier, nchan - 1 + jnp.minimum(place, 1) + jnp.minimum(last - place, 1)
    )

    other = {"rep": 1 - rep}
    depth = D // nrep
    rows_r = PATCH // nrep
    here_r = pl.ds(pl.multiple_of(rep * rows_r, rows_r), rows_r)
    here_d = pl.ds(pl.multiple_of(rep * depth, depth), depth)
    there_r = pl.ds(pl.multiple_of((1 - rep) * rows_r, rows_r), rows_r)
    there_d = pl.ds(pl.multiple_of((1 - rep) * depth, depth), depth)
    moves = [
        (pw_ref.at[:, 0], lambda rows, _: wp.at[0, rows]),
        (pw_ref.at[:, 1], lambda rows, _: wp.at[1, rows]),
        (vw_ref, lambda _, rows: wv.at[rows]),
        (ow_ref, lambda _, rows: wo.at[rows]),
    ]

    def local_weight(n):
        source, target = moves[n]
        return pltpu.make_async_copy(source, target(here_r, here_d), w_local.at[n])

    def remote_weight(n, rows_r_, rows_d_):
        source, target = moves[n]
        return pltpu.make_async_remote_copy(
            src_ref=source, dst_ref=target(rows_r_, rows_d_),
            send_sem=w_send.at[n], recv_sem=w_recv.at[n],
            device_id=other, device_id_type=MESH,
        )

    def remote_decoder(rows):
        return pltpu.make_async_remote_copy(
            src_ref=wd.at[rows], dst_ref=wd.at[rows],
            send_sem=w_send.at[len(moves)], recv_sem=w_recv.at[len(moves)],
            device_id=other, device_id_type=MESH,
        )

    for n in range(len(moves)):
        local_weight(n).start()
        remote_weight(n, here_r, here_d).start()

    def wait_weight(n):
        local_weight(n).wait()
        remote_weight(n, here_r, here_d).wait_send()
        remote_weight(n, there_r, there_d).wait_recv()

    lane = iota((LANES, D), 0)
    feature = lax.shift_right_logical(iota((LANES, D), 1), 6)
    expand[...] = jnp.where(
        (lax.shift_right_logical(lane, 3) == feature) & ((lane & (COPIES - 1)) < 3), 1.0, 0.0
    ).astype(BF16)

    def span(g):
        return pl.ds(pl.multiple_of(g * group, group), group)

    def bundle(p):
        return pl.ds(pl.multiple_of(p * pack, pack), pack)

    def places(p):
        return pl.ds(pl.multiple_of(p * CHUNK, CHUNK), CHUNK)

    every = pl.ds(0, chans)

    def halo_up(s, n, first, count, which=every):
        return pltpu.make_async_remote_copy(
            src_ref=patches.at[s, pl.ds(first, count), which, LANES : 2 * LANES],
            dst_ref=patches.at[s, pl.ds(first, count), which, 3 * LANES :],
            send_sem=h_send.at[s, 0, n], recv_sem=h_recv.at[s, 1, n],
            device_id=up, device_id_type=MESH,
        )

    def halo_down(s, n, first, count, which=every):
        return pltpu.make_async_remote_copy(
            src_ref=patches.at[s, pl.ds(first, count), which, 2 * LANES : 3 * LANES],
            dst_ref=patches.at[s, pl.ds(first, count), which, :LANES],
            send_sem=h_send.at[s, 1, n], recv_sem=h_recv.at[s, 0, n],
            device_id=down, device_id_type=MESH,
        )

    def rim_up(s, n):
        return pltpu.make_async_remote_copy(
            src_ref=rim_out.at[s, 0, n], dst_ref=rim_in.at[s, 1, n],
            send_sem=r_send.at[s, 0, n], recv_sem=r_recv.at[s, 1, n],
            device_id=up, device_id_type=MESH,
        )

    def rim_down(s, n):
        return pltpu.make_async_remote_copy(
            src_ref=rim_out.at[s, 1, n], dst_ref=rim_in.at[s, 0, n],
            send_sem=r_send.at[s, 1, n], recv_sem=r_recv.at[s, 0, n],
            device_id=down, device_id_type=MESH,
        )

    def edge_up(s):
        return pltpu.make_async_remote_copy(
            src_ref=edge_out.at[s, 0], dst_ref=edge_in.at[s, 1],
            send_sem=r_send.at[s, 0, nchunks], recv_sem=r_recv.at[s, 1, nchunks],
            device_id=up, device_id_type=MESH,
        )

    def edge_down(s):
        return pltpu.make_async_remote_copy(
            src_ref=edge_out.at[s, 1], dst_ref=edge_in.at[s, 0],
            send_sem=r_send.at[s, 1, nchunks], recv_sem=r_recv.at[s, 0, nchunks],
            device_id=down, device_id_type=MESH,
        )

    seam = my_chunk * CHUNK

    def fill_own(s, p):
        patches[s, pl.ds(0, cols), bundle(p), LANES : 3 * LANES] = state[:, bundle(p), :].astype(BF16)

    def first_of(chunk):
        return 2 * chunk, chunk * CHUNK, 1

    def rest_of(chunk):
        return 2 * chunk + 1, chunk * CHUNK + 1, CHUNK - 1

    def send_halo(s, piece, which=every):
        @pl.when(has_up)
        def _():
            halo_up(s, *piece, which).start()

        @pl.when(has_down)
        def _():
            halo_down(s, *piece, which).start()

    def wait_halo(s, piece):
        @pl.when(has_up)
        def _():
            halo_up(s, *piece).wait_send()
            halo_down(s, *piece).wait_recv()

        @pl.when(has_down)
        def _():
            halo_down(s, *piece).wait_send()
            halo_up(s, *piece).wait_recv()

    for t in range(tiles_across):
        load(t).wait()

    @pl.loop(0, packs)
    def _(p):
        @pl.loop(0, ratio)
        def _(i):
            g = p * ratio + i

            @pl.loop(0, 2)
            def _(half):
                first = g * (group * STRIDE) + half * 8
                fields = [
                    pltpu.roll(
                        jnp.concatenate(
                            [
                                pixels_in[t, pl.ds(first + r, group, stride=STRIDE), :]
                                for t in range(tiles_across)
                            ],
                            axis=1,
                        ),
                        RIM, 1,
                    )
                    for r in range(8)
                ]
                there = pl.ds(pl.multiple_of(half * LANES, LANES), LANES)
                for t in range(cols // 8):
                    tiles = swap_chunks([field[:, t * LANES : (t + 1) * LANES] for field in fields])
                    for j in range(8):
                        state[t * 8 + j, span(g), there] = tiles[j]

        fill_own(0, p)

        @pl.loop(0, nchunks)
        def _(i):
            chunk = (my_chunk + 1 + i) % nchunks
            send_halo(0, first_of(chunk), bundle(p))
            send_halo(0, rest_of(chunk), bundle(p))

    source = iota((2 * LANES, 2 * LANES), 0)
    target = iota((2 * LANES, 2 * LANES), 1)
    moved = (
        (lax.shift_right_logical(source, 4) & 1) * LANES
        + lax.shift_right_logical(source, 5) * STRIDE
        + (source & (STRIDE - 1))
    )
    order = jnp.where(moved == target, 1.0, 0.0).astype(BF16)
    for b in range(D // (2 * LANES)):
        ordered = jnp.dot(
            dw_ref[:, b * 2 * LANES : (b + 1) * 2 * LANES], order, preferred_element_type=F32
        )
        ordered = (0.25 * ordered).astype(BF16)
        wd[here_d, b * LANES : (b + 1) * LANES] = ordered[:, :LANES]
        wd[here_d, D // 2 + b * LANES : D // 2 + (b + 1) * LANES] = ordered[:, LANES:]
    remote_decoder(here_d).start()

    zeros = jnp.zeros((STEPS, cols, chans, LANES), BF16)

    @pl.when(jnp.logical_not(has_up))
    def _():
        patches[:, :cols, :, :LANES] = zeros

    @pl.when(jnp.logical_not(has_down))
    def _():
        patches[:, :cols, :, 3 * LANES :] = zeros

    spots = jnp.where(
        lax.shift_right_logical(iota((LANES, HEADS), 0), 3) == iota((LANES, HEADS), 1), 1.0, 0.0
    ).astype(BF16)
    keys[...] = jnp.dot(spots, qk_ref[...], preferred_element_type=F32).astype(BF16)

    for n in range(3):
        wait_weight(n)

    def part_copy(s, to, slot):
        return pltpu.make_async_remote_copy(
            src_ref=part_out.at[s, to // owners], dst_ref=part_in.at[s, slot],
            send_sem=p_send.at[s, to], recv_sem=p_recv.at[s, slot],
            device_id={"chan": to}, device_id_type=MESH,
        )

    def mixed_copy(s, chunk, slot):
        return pltpu.make_async_remote_copy(
            src_ref=mixed.at[s, my_chunk], dst_ref=mixed.at[s, slot],
            send_sem=m_send.at[s, chunk], recv_sem=m_recv.at[s, slot],
            device_id={"chan": chunk * owners + my_lane}, device_id_type=MESH,
        )

    def store(n, first, count):
        return pltpu.make_async_copy(
            state.at[pl.ds(first, count)], out_ref.at[pl.ds(first, count)], out_sem.at[n]
        )

    span_rows = COPIES * chans

    def embed(s, chunk, slot):
        start = pl.multiple_of(chunk * CHUNK, CHUNK)
        rows = jnp.concatenate(
            [patches[s, pl.ds(start, CHUNK)], patches[s, pl.ds(start + 1, CHUNK)]], axis=2
        ).reshape(CHUNK * chans, D)
        embedded = jnp.dot(rows, wp[...].reshape(D, D), preferred_element_type=F32)
        embedded = embedded.reshape(CHUNK, chans, D) + ce_ref[...][None]
        tokens[slot][...] = embedded.astype(BF16).reshape(CHUNK * chans, D)

    def aggregate(s, chunk, slot):
        for r in range(0, CHUNK * chans, 16):
            normed[r : r + 16] = normalize(tokens[slot][r : r + 16].astype(F32))
        scores = lax.dot_general(
            normed[...], keys[...], (((1,), (1,)), ((), ())), preferred_element_type=F32
        )
        scores = scores.reshape(CHUNK, chans, LANES)
        peak = jnp.max(scores, axis=1, keepdims=True)
        raised = jnp.exp(scores - peak).astype(BF16).astype(F32)
        part_out[s, chunk, :, D : D + LANES] = jnp.max(scores, axis=1)
        part_out[s, chunk, :, D + LANES :] = jnp.sum(raised, axis=1)
        own = (iota(raised.shape, 2) & (COPIES - 1)) == (iota(raised.shape, 0) & (COPIES - 1))
        placed = jnp.where(own, raised, 0.0).reshape(CHUNK * chans, LANES)
        highs, lows = [], []
        for k in range(CHUNK // COPIES):
            rows = slice(k * span_rows, (k + 1) * span_rows)
            total = jnp.dot(placed[rows].T.astype(BF16), normed[rows], preferred_element_type=F32)
            high = total.astype(BF16)
            highs.append(high)
            lows.append((total - high.astype(F32)).astype(BF16))
        depth_n = WIDE // HEAD_DIM * COPIES
        head = lax.shift_right_logical(iota((COPIES, WIDE), 1), 6)
        for n in range(D // WIDE):
            rows = slice(n * depth_n, (n + 1) * depth_n)
            columns = slice(n * WIDE, (n + 1) * WIDE)
            mixed_heads = jnp.dot(
                jnp.concatenate([part[rows] for part in highs + lows], axis=0),
                wv[:, columns], preferred_element_type=F32,
            )
            for k in range(CHUNK // COPIES):
                low = (CHUNK // COPIES + k) * depth_n
                both = mixed_heads[k * depth_n : (k + 1) * depth_n] + mixed_heads[low : low + depth_n]
                kept = both[:COPIES]
                for h in range(1, WIDE // HEAD_DIM):
                    kept = jnp.where(head == h, both[h * COPIES : (h + 1) * COPIES], kept)
                part_out[s, chunk, k * COPIES : (k + 1) * COPIES, columns] = kept

    def step(s):
        order = [(my_chunk + 1 + i) % nchunks for i in range(nchunks)]
        wait_halo(s, first_of(order[0]))
        for i in range(nchunks + 1):
            if i < nchunks:
                wait_halo(s, rest_of(order[i]))
                if i + 1 < nchunks:
                    wait_halo(s, first_of(order[i + 1]))

                @pl.when(order[i] == nchunks - 1)
                def _():
                    patches[s, cols] = patches[s, 0]

                embed(s, order[i], i % 2)
            if i > 0:
                aggregate(s, order[i - 1], (i - 1) % 2)

                @pl.loop(0, owners)
                def _(a):
                    to = order[i - 1] * owners + a

                    @pl.when(to != me)
                    def _():
                        part_copy(s, to, me).start()

        part_in[s, me] = part_out[s, my_chunk]

        @pl.when(s == 0)
        def _():
            wait_weight(3)

        @pl.loop(1, nchan)
        def _(i):
            peer = (me + i) % nchan
            part_copy(s, peer, me).wait_send()
            part_copy(s, peer, peer).wait_recv()

        peaks = part_in[s, :, :, D : D + LANES]
        factors = jnp.exp(peaks - jnp.max(peaks, axis=0)[None])
        total = jnp.sum(factors * part_in[s, :, :, D + LANES :], axis=0)
        factors = factors / total[None]
        factors = jnp.dot(
            split_parts(factors.reshape(nchan * CHUNK, LANES)), expand[...], preferred_element_type=F32
        ).reshape(nchan, CHUNK, D)
        blended = jnp.sum(factors * part_in[s, :, :, :D], axis=0).astype(BF16)
        mixed[s, my_chunk] = jnp.dot(blended, wo[...], preferred_element_type=F32).astype(BF16)

        @pl.loop(1, nchunks)
        def _(i):
            mixed_copy(s, (my_chunk + nchunks - i) % nchunks, my_chunk).start()

        @pl.when(s == 0)
        def _():
            remote_decoder(here_d).wait_send()
            remote_decoder(there_d).wait_recv()

        carry[...] = jnp.zeros_like(carry)

        @pl.loop(0, nchunks + LAG)
        def _(i):
            @pl.when(i < nchunks)
            def _():
                chunk = (my_chunk + i) % nchunks

                @pl.when(i > 0)
                def _():
                    mixed_copy(s, chunk, my_chunk).wait_send()
                    mixed_copy(s, chunk, chunk).wait_recv()

                rows = mixed[s, chunk].astype(F32)
                for j in range(CHUNK):
                    mixed_rows[j] = jnp.broadcast_to(rows[j : j + 1], (group, D))
                hidden = gelu(
                    mixed_rows[...][:, None] + de_ref[...].reshape(groups, group, D)[None]
                ).reshape(CHUNK * chans, D).astype(BF16)
                pixels = jnp.dot(hidden, wd[...], preferred_element_type=F32).reshape(CHUNK, chans, D)
                right = pixels[:, :, D // 2 :]
                blocks = pixels[:, :, : D // 2] + jnp.concatenate([carry[...][None], right[:-1]], axis=0)
                carry[...] = right[CHUNK - 1]
                rim_out[s, 0, chunk] = blocks[:, :, :LANES].astype(BF16)
                rim_out[s, 1, chunk] = blocks[:, :, 3 * LANES :].astype(BF16)

                @pl.when(has_up)
                def _():
                    rim_up(s, chunk).start()

                @pl.when(has_down)
                def _():
                    rim_down(s, chunk).start()

                state[places(chunk)] = state[places(chunk)] + blocks[:, :, LANES : 3 * LANES]

                @pl.when(i == nchunks - 1)
                def _():
                    edge_out[s, 0] = carry[:, :LANES].astype(BF16)
                    edge_out[s, 1] = carry[:, 3 * LANES :].astype(BF16)

                    @pl.when(has_up)
                    def _():
                        edge_up(s).start()

                    @pl.when(has_down)
                    def _():
                        edge_down(s).start()

                    state[seam] = state[seam] + carry[:, LANES : 3 * LANES]

            @pl.when(i >= LAG)
            def _():
                chunk = (my_chunk + i - LAG) % nchunks

                @pl.when(has_up)
                def _():
                    rim_up(s, chunk).wait_send()
                    rim_down(s, chunk).wait_recv()
                    state[places(chunk), :, :LANES] = (
                        state[places(chunk), :, :LANES] + rim_in[s, 0, chunk].astype(F32)
                    )

                @pl.when(has_down)
                def _():
                    rim_down(s, chunk).wait_send()
                    rim_up(s, chunk).wait_recv()
                    state[places(chunk), :, LANES:] = (
                        state[places(chunk), :, LANES:] + rim_in[s, 1, chunk].astype(F32)
                    )

                @pl.when(s < STEPS - 1)
                def _():
                    patches[s + 1, places(chunk), :, LANES : 3 * LANES] = state[places(chunk)].astype(BF16)

                    @pl.when(i == LAG)
                    def _():
                        send_halo(s + 1, rest_of(my_chunk))

                    @pl.when(i > LAG)
                    def _():
                        send_halo(s + 1, first_of(chunk))
                        send_halo(s + 1, rest_of(chunk))

                @pl.when(s == STEPS - 1)
                def _():
                    @pl.when(i == LAG)
                    def _():
                        store(my_chunk, seam + 1, CHUNK - 1).start()

                    @pl.when(i > LAG)
                    def _():
                        store(chunk, chunk * CHUNK, CHUNK).start()

        @pl.when(has_up)
        def _():
            edge_up(s).wait_send()
            edge_down(s).wait_recv()
            state[seam, :, :LANES] = state[seam, :, :LANES] + edge_in[s, 0].astype(F32)

        @pl.when(has_down)
        def _():
            edge_down(s).wait_send()
            edge_up(s).wait_recv()
            state[seam, :, LANES:] = state[seam, :, LANES:] + edge_in[s, 1].astype(F32)

        @pl.when(s < STEPS - 1)
        def _():
            patches[s + 1, seam, :, LANES : 3 * LANES] = state[seam].astype(BF16)
            send_halo(s + 1, first_of(my_chunk))

    @pl.loop(0, STEPS)
    def _(s):
        step(s)

    store(nchunks, seam, 1).start()
    store(my_chunk, seam + 1, CHUNK - 1).wait()
    for i in range(1, nchunks):
        chunk = (my_chunk + i) % nchunks
        store(chunk, chunk * CHUNK, CHUNK).wait()
    store(nchunks, seam, 1).wait()


def lay_kernel(chans, cols, blocks_ref, out_ref, held, pixels_out, in_sem, out_sem):
    group = min(8, chans)
    groups = chans // group
    tiles_across = cols // 8

    def load(g):
        return pltpu.make_async_copy(
            blocks_ref.at[:, pl.ds(pl.multiple_of(g * group, group), group)], held.at[g], in_sem.at[g]
        )

    def store(g, t):
        rows = pl.ds(pl.multiple_of(g * (group * STRIDE), group * STRIDE), group * STRIDE)
        return pltpu.make_async_copy(
            pixels_out.at[t, rows], out_ref.at[rows, t * LANES : (t + 1) * LANES], out_sem.at[g, t]
        )

    for g in range(groups):
        load(g).start()

    @pl.loop(0, groups)
    def _(g):
        load(g).wait()

        @pl.loop(0, 2)
        def _(half):
            first = g * (group * STRIDE) + half * 8
            there = pl.ds(pl.multiple_of(half * LANES, LANES), LANES)
            columns = [
                swap_chunks([held[g, t * 8 + j, :, there] for j in range(8)]) for t in range(cols // 8)
            ]
            for r in range(8):
                field = jnp.concatenate([tiles[r] for tiles in columns], axis=1)
                field = pltpu.roll(field, field.shape[1] - RIM, 1)
                for t in range(tiles_across):
                    pixels_out[t, pl.ds(first + r, group, stride=STRIDE), :] = field[
                        :, t * LANES : (t + 1) * LANES
                    ]

        for t in range(tiles_across):
            store(g, t).start()

    @pl.loop(0, groups)
    def _(g):
        for t in range(tiles_across):
            store(g, t).wait()


def body(mesh_sizes, state_field, patch_weight, chan_embed, query_keys, value_weight, out_weight, dec_embed, dec_weight):
    nchan, nband, nrep = mesh_sizes
    chans, rows, width = state_field.shape
    cols = width // STRIDE
    group = min(8, chans)
    groups = chans // group
    nchunks = cols // CHUNK
    assert rows == STRIDE and nrep == 2 and nchan % nchunks == 0
    vmem = pl.BlockSpec(memory_space=pltpu.VMEM)
    whole = pl.BlockSpec(memory_space=pl.ANY)
    dma = pltpu.SemaphoreType.DMA
    blocks = pl.pallas_call(
        functools.partial(kernel, (chans, cols, nchan, nband, nrep)),
        out_shape=jax.ShapeDtypeStruct((cols, chans, 2 * LANES), F32),
        in_specs=[whole, whole, vmem, vmem, whole, whole, vmem, vmem],
        out_specs=whole,
        scratch_shapes=[
            pltpu.VMEM((cols, chans, 2 * LANES), F32),
            pltpu.VMEM((STEPS, cols + 1, chans, D // 2), BF16),
            pltpu.VMEM((2, PATCH, STRIDE, D), BF16),
            pltpu.VMEM((D, D), BF16),
            pltpu.VMEM((D, D), BF16),
            pltpu.VMEM((D, D), BF16),
            pltpu.VMEM((LANES, D), BF16),
            pltpu.VMEM((LANES, D), BF16),
            pltpu.VMEM((CHUNK, group, D), F32),
            pltpu.VMEM((cols // 8, chans * rows, LANES), F32),
            pltpu.VMEM((STEPS, 2, nchunks, CHUNK, chans, LANES), BF16),
            pltpu.VMEM((STEPS, 2, nchunks, CHUNK, chans, LANES), BF16),
            pltpu.VMEM((STEPS, 2, chans, LANES), BF16),
            pltpu.VMEM((STEPS, 2, chans, LANES), BF16),
            pltpu.VMEM((chans, D // 2), F32),
            pltpu.VMEM((STEPS, nchunks, CHUNK, PACKET), F32),
            pltpu.VMEM((STEPS, nchan, CHUNK, PACKET), F32),
            pltpu.VMEM((STEPS, nchunks, CHUNK, D), BF16),
            pltpu.VMEM((CHUNK * chans, D), BF16),
            pltpu.VMEM((CHUNK * chans, D), BF16),
            pltpu.VMEM((CHUNK * chans, D), BF16),
            dma((cols // 8,)), dma((nchunks + 1,)), dma((4,)), dma((5,)), dma((5,)),
            dma((STEPS, 2, 2 * nchunks)), dma((STEPS, 2, 2 * nchunks)),
            dma((STEPS, 2, nchunks + 1)), dma((STEPS, 2, nchunks + 1)),
            dma((STEPS, nchan)), dma((STEPS, nchan)),
            dma((STEPS, nchunks)), dma((STEPS, nchunks)),
        ],
        compiler_params=pltpu.CompilerParams(
            collective_id=0, has_side_effects=True, vmem_limit_bytes=60 * 1024 * 1024
        ),
        name="rollout",
    )(
        state_field.reshape(chans * rows, width),
        patch_weight.reshape(PATCH // nrep, 2, STRIDE, D),
        chan_embed,
        query_keys.T,
        value_weight,
        out_weight,
        dec_embed,
        dec_weight,
    )
    return pl.pallas_call(
        functools.partial(lay_kernel, chans, cols),
        out_shape=jax.ShapeDtypeStruct((chans * rows, width), F32),
        in_specs=[whole],
        out_specs=whole,
        scratch_shapes=[
            pltpu.VMEM((groups, cols, group, 2 * LANES), F32),
            pltpu.VMEM((cols // 8, chans * rows, LANES), F32),
            dma((groups,)), dma((groups, cols // 8)),
        ],
        compiler_params=pltpu.CompilerParams(vmem_limit_bytes=60 * 1024 * 1024),
        name="lay",
    )(blocks).reshape(state_field.shape)


def solution(mesh):
    in_specs = (
        P(("groups", "chan"), ("band", "rep"), None),
        P("rep", None),
        P("chan", None),
        P(),
        P("rep", None),
        P("rep", None),
        P("chan", None),
        P("rep", None),
    )
    out_specs = P(("groups", "chan"), ("band", "rep"), None)
    sizes = (mesh.shape["chan"], mesh.shape["band"], mesh.shape["rep"])
    return jax.shard_map(
        functools.partial(body, sizes), mesh=mesh, in_specs=in_specs, out_specs=out_specs, check_vma=False
    )
```

```python
import functools

import jax
import jax.numpy as jnp
from jax import lax
from jax.experimental import pallas as pl
from jax.experimental.pallas import tpu as pltpu
from jax.sharding import PartitionSpec as P

D = 1024
HEADS = 16
HEAD_DIM = D // HEADS
PATCH = 32
STRIDE = 16
RIM = 8
STEPS = 2
LANES = 128
COPIES = LANES // HEADS
CHUNK = 16
WIDE = 256
LAG = 3
PACKET = D + 2 * LANES
MESH = pl.DeviceIdType.MESH
F32 = jnp.float32
BF16 = jnp.bfloat16


def iota(shape, dim):
    return lax.broadcasted_iota(jnp.int32, shape, dim)


def swap_chunks(tiles):
    tiles = list(tiles)
    chunk = lax.shift_right_logical(iota(tiles[0].shape, 1), 4)
    for bit in (1, 2, 4):
        high = (chunk & bit) != 0
        for low in range(8):
            if low & bit:
                continue
            first, second = tiles[low], tiles[low + bit]
            if bit == 4:
                moved = pltpu.roll(jnp.where(high, first, second), LANES // 2, 1)
                tiles[low] = jnp.where(high, moved, first)
                tiles[low + bit] = jnp.where(high, second, moved)
                continue
            tiles[low] = jnp.where(high, pltpu.roll(second, 16 * bit, 1), first)
            tiles[low + bit] = jnp.where(high, second, pltpu.roll(first, LANES - 16 * bit, 1))
    return tiles


def trade_chunks(tiles):
    tiles = list(tiles)
    lane = iota(tiles[0].shape, 1)
    chunk = lax.shift_right_logical(lane, 4)
    for bit in (1, 2, 4):
        high = (chunk & bit) != 0
        for low in range(8):
            if low & bit:
                continue
            first, second = tiles[low], tiles[low + bit]
            moved = jnp.where(high, first, second)
            if bit == 4:
                moved = pltpu.roll(moved, LANES // 2, 1)
            else:
                moved = jnp.take_along_axis(moved, lane ^ (16 * bit), axis=1)
            tiles[low] = jnp.where(high, moved, first)
            tiles[low + bit] = jnp.where(high, second, moved)
    return tiles


def split_parts(values):
    high = values.astype(BF16)
    rest = values - high.astype(F32)
    middle = rest.astype(BF16)
    low = (rest - middle.astype(F32)).astype(BF16)
    copy = iota(values.shape, values.ndim - 1) & (COPIES - 1)
    parts = jnp.where(copy == 0, high.astype(F32), jnp.where(copy == 1, middle.astype(F32), low.astype(F32)))
    return jnp.where(copy < 3, parts, 0.0).astype(BF16)


def normalize(tokens):
    centre = jnp.mean(tokens, axis=-1, keepdims=True)
    moved = tokens - centre
    spread = jnp.mean(jnp.square(moved), axis=-1, keepdims=True)
    return (moved * lax.rsqrt(spread + 1e-05)).astype(BF16)


def gelu(x):
    return 0.5 * x * (1.0 + lax.erf(x * 0.7071067811865476))


def kernel(
    sizes,
    x_ref, pw_ref, ce_ref, qk_ref, vw_ref, ow_ref, de_ref, dw_ref,
    out_ref,
    state, patches, wp, wv, wo, wd, expand, keys, mixed_rows,
    pixels_in, rim_out, rim_in, edge_out, edge_in, carry, part_out, part_in, mixed,
    tokens_a, tokens_b, normed,
    x_sem, out_sem, w_local, w_send, w_recv, h_send, h_recv, r_send, r_recv, p_send, p_recv, m_send, m_recv,
):
    chans, cols, nchan, nband, nrep = sizes
    tokens = (tokens_a, tokens_b)
    group = min(8, chans)
    groups = chans // group
    pack = min(16, chans)
    ratio = pack // group
    packs = chans // pack
    nchunks = cols // CHUNK
    owners = nchan // nchunks
    me = lax.axis_index("chan")
    rep = lax.axis_index("rep")
    place = lax.axis_index("band") * nrep + rep
    last = nband * nrep - 1
    has_up = place > 0
    has_down = place < last
    up_place = jnp.maximum(place - 1, 0)
    down_place = jnp.minimum(place + 1, last)
    up = {"band": up_place // nrep, "rep": up_place % nrep}
    down = {"band": down_place // nrep, "rep": down_place % nrep}
    my_chunk = me // owners
    my_lane = me % owners

    tiles_across = cols // 8

    def load(t):
        return pltpu.make_async_copy(
            x_ref.at[:, t * LANES : (t + 1) * LANES], pixels_in.at[t], x_sem.at[t]
        )

    for t in range(tiles_across):
        load(t).start()

    barrier = pltpu.get_barrier_semaphore()

    @pl.when(has_up)
    def _():
        pl.semaphore_signal(barrier, inc=1, device_id=up, device_id_type=MESH)

    @pl.when(has_down)
    def _():
        pl.semaphore_signal(barrier, inc=1, device_id=down, device_id_type=MESH)

    @pl.loop(1, nchan)
    def _(i):
        pl.semaphore_signal(
            barrier, inc=1, device_id={"chan": (me + i) % nchan}, device_id_type=MESH
        )

    pl.semaphore_wait(
        barrier, nchan - 1 + jnp.minimum(place, 1) + jnp.minimum(last - place, 1)
    )

    other = {"rep": 1 - rep}
    depth = D // nrep
    rows_r = PATCH // nrep
    here_r = pl.ds(pl.multiple_of(rep * rows_r, rows_r), rows_r)
    here_d = pl.ds(pl.multiple_of(rep * depth, depth), depth)
    there_r = pl.ds(pl.multiple_of((1 - rep) * rows_r, rows_r), rows_r)
    there_d = pl.ds(pl.multiple_of((1 - rep) * depth, depth), depth)
    moves = [
        (pw_ref.at[:, 0], lambda rows, _: wp.at[0, rows]),
        (pw_ref.at[:, 1], lambda rows, _: wp.at[1, rows]),
        (vw_ref, lambda _, rows: wv.at[rows]),
        (ow_ref, lambda _, rows: wo.at[rows]),
    ]

    def local_weight(n):
        source, target = moves[n]
        return pltpu.make_async_copy(source, target(here_r, here_d), w_local.at[n])

    def remote_weight(n, rows_r_, rows_d_):
        source, target = moves[n]
        return pltpu.make_async_remote_copy(
            src_ref=source, dst_ref=target(rows_r_, rows_d_),
            send_sem=w_send.at[n], recv_sem=w_recv.at[n],
            device_id=other, device_id_type=MESH,
        )

    def remote_decoder(rows):
        return pltpu.make_async_remote_copy(
            src_ref=wd.at[rows], dst_ref=wd.at[rows],
            send_sem=w_send.at[len(moves)], recv_sem=w_recv.at[len(moves)],
            device_id=other, device_id_type=MESH,
        )

    for n in range(len(moves)):
        local_weight(n).start()
        remote_weight(n, here_r, here_d).start()

    def wait_weight(n):
        local_weight(n).wait()
        remote_weight(n, here_r, here_d).wait_send()
        remote_weight(n, there_r, there_d).wait_recv()

    lane = iota((LANES, D), 0)
    feature = lax.shift_right_logical(iota((LANES, D), 1), 6)
    expand[...] = jnp.where(
        (lax.shift_right_logical(lane, 3) == feature) & ((lane & (COPIES - 1)) < 3), 1.0, 0.0
    ).astype(BF16)

    def span(g):
        return pl.ds(pl.multiple_of(g * group, group), group)

    def bundle(p):
        return pl.ds(pl.multiple_of(p * pack, pack), pack)

    def places(p):
        return pl.ds(pl.multiple_of(p * CHUNK, CHUNK), CHUNK)

    every = pl.ds(0, chans)

    def halo_up(s, n, first, count, which=every):
        return pltpu.make_async_remote_copy(
            src_ref=patches.at[s, pl.ds(first, count), which, LANES : 2 * LANES],
            dst_ref=patches.at[s, pl.ds(first, count), which, 3 * LANES :],
            send_sem=h_send.at[s, 0, n], recv_sem=h_recv.at[s, 1, n],
            device_id=up, device_id_type=MESH,
        )

    def halo_down(s, n, first, count, which=every):
        return pltpu.make_async_remote_copy(
            src_ref=patches.at[s, pl.ds(first, count), which, 2 * LANES : 3 * LANES],
            dst_ref=patches.at[s, pl.ds(first, count), which, :LANES],
            send_sem=h_send.at[s, 1, n], recv_sem=h_recv.at[s, 0, n],
            device_id=down, device_id_type=MESH,
        )

    def rim_up(s, n):
        return pltpu.make_async_remote_copy(
            src_ref=rim_out.at[s, 0, n], dst_ref=rim_in.at[s, 1, n],
            send_sem=r_send.at[s, 0, n], recv_sem=r_recv.at[s, 1, n],
            device_id=up, device_id_type=MESH,
        )

    def rim_down(s, n):
        return pltpu.make_async_remote_copy(
            src_ref=rim_out.at[s, 1, n], dst_ref=rim_in.at[s, 0, n],
            send_sem=r_send.at[s, 1, n], recv_sem=r_recv.at[s, 0, n],
            device_id=down, device_id_type=MESH,
        )

    def edge_up(s):
        return pltpu.make_async_remote_copy(
            src_ref=edge_out.at[s, 0], dst_ref=edge_in.at[s, 1],
            send_sem=r_send.at[s, 0, nchunks], recv_sem=r_recv.at[s, 1, nchunks],
            device_id=up, device_id_type=MESH,
        )

    def edge_down(s):
        return pltpu.make_async_remote_copy(
            src_ref=edge_out.at[s, 1], dst_ref=edge_in.at[s, 0],
            send_sem=r_send.at[s, 1, nchunks], recv_sem=r_recv.at[s, 0, nchunks],
            device_id=down, device_id_type=MESH,
        )

    seam = my_chunk * CHUNK

    def fill_own(s, p):
        patches[s, pl.ds(0, cols), bundle(p), LANES : 3 * LANES] = state[:, bundle(p), :].astype(BF16)

    def first_of(chunk):
        return 2 * chunk, chunk * CHUNK, 1

    def rest_of(chunk):
        return 2 * chunk + 1, chunk * CHUNK + 1, CHUNK - 1

    def send_halo(s, piece, which=every):
        @pl.when(has_up)
        def _():
            halo_up(s, *piece, which).start()

        @pl.when(has_down)
        def _():
            halo_down(s, *piece, which).start()

    def wait_halo(s, piece):
        @pl.when(has_up)
        def _():
            halo_up(s, *piece).wait_send()
            halo_down(s, *piece).wait_recv()

        @pl.when(has_down)
        def _():
            halo_down(s, *piece).wait_send()
            halo_up(s, *piece).wait_recv()

    for t in range(tiles_across):
        load(t).wait()

    @pl.loop(0, packs)
    def _(p):
        @pl.loop(0, ratio)
        def _(i):
            g = p * ratio + i

            @pl.loop(0, 2)
            def _(half):
                first = g * (group * STRIDE) + half * 8
                fields = [
                    pltpu.roll(
                        jnp.concatenate(
                            [
                                pixels_in[t, pl.ds(first + r, group, stride=STRIDE), :]
                                for t in range(tiles_across)
                            ],
                            axis=1,
                        ),
                        RIM, 1,
                    )
                    for r in range(8)
                ]
                there = pl.ds(pl.multiple_of(half * LANES, LANES), LANES)
                for t in range(cols // 8):
                    tiles = trade_chunks([field[:, t * LANES : (t + 1) * LANES] for field in fields])
                    for j in range(8):
                        state[t * 8 + j, span(g), there] = tiles[j]

        fill_own(0, p)

        @pl.loop(0, nchunks)
        def _(i):
            chunk = (my_chunk + 1 + i) % nchunks
            send_halo(0, first_of(chunk), bundle(p))
            send_halo(0, rest_of(chunk), bundle(p))

    source = iota((2 * LANES, 2 * LANES), 0)
    target = iota((2 * LANES, 2 * LANES), 1)
    moved = (
        (lax.shift_right_logical(source, 4) & 1) * LANES
        + lax.shift_right_logical(source, 5) * STRIDE
        + (source & (STRIDE - 1))
    )
    order = jnp.where(moved == target, 1.0, 0.0).astype(BF16)
    for b in range(D // (2 * LANES)):
        ordered = jnp.dot(
            dw_ref[:, b * 2 * LANES : (b + 1) * 2 * LANES], order, preferred_element_type=F32
        )
        ordered = (0.25 * ordered).astype(BF16)
        wd[here_d, b * LANES : (b + 1) * LANES] = ordered[:, :LANES]
        wd[here_d, D // 2 + b * LANES : D // 2 + (b + 1) * LANES] = ordered[:, LANES:]
    remote_decoder(here_d).start()

    zeros = jnp.zeros((STEPS, cols, chans, LANES), BF16)

    @pl.when(jnp.logical_not(has_up))
    def _():
        patches[:, :cols, :, :LANES] = zeros

    @pl.when(jnp.logical_not(has_down))
    def _():
        patches[:, :cols, :, 3 * LANES :] = zeros

    spots = jnp.where(
        lax.shift_right_logical(iota((LANES, HEADS), 0), 3) == iota((LANES, HEADS), 1), 1.0, 0.0
    ).astype(BF16)
    keys[...] = jnp.dot(spots, qk_ref[...], preferred_element_type=F32).astype(BF16)

    for n in range(3):
        wait_weight(n)

    def part_copy(s, to, slot):
        return pltpu.make_async_remote_copy(
            src_ref=part_out.at[s, to // owners], dst_ref=part_in.at[s, slot],
            send_sem=p_send.at[s, to], recv_sem=p_recv.at[s, slot],
            device_id={"chan": to}, device_id_type=MESH,
        )

    def mixed_copy(s, chunk, slot):
        return pltpu.make_async_remote_copy(
            src_ref=mixed.at[s, my_chunk], dst_ref=mixed.at[s, slot],
            send_sem=m_send.at[s, chunk], recv_sem=m_recv.at[s, slot],
            device_id={"chan": chunk * owners + my_lane}, device_id_type=MESH,
        )

    def store(n, first, count):
        return pltpu.make_async_copy(
            state.at[pl.ds(first, count)], out_ref.at[pl.ds(first, count)], out_sem.at[n]
        )

    span_rows = COPIES * chans

    def embed(s, chunk, slot):
        start = pl.multiple_of(chunk * CHUNK, CHUNK)
        rows = jnp.concatenate(
            [patches[s, pl.ds(start, CHUNK)], patches[s, pl.ds(start + 1, CHUNK)]], axis=2
        ).reshape(CHUNK * chans, D)
        embedded = jnp.dot(rows, wp[...].reshape(D, D), preferred_element_type=F32)
        embedded = embedded.reshape(CHUNK, chans, D) + ce_ref[...][None]
        tokens[slot][...] = embedded.astype(BF16).reshape(CHUNK * chans, D)

    def aggregate(s, chunk, slot):
        for r in range(0, CHUNK * chans, 16):
            normed[r : r + 16] = normalize(tokens[slot][r : r + 16].astype(F32))
        scores = lax.dot_general(
            normed[...], keys[...], (((1,), (1,)), ((), ())), preferred_element_type=F32
        )
        scores = scores.reshape(CHUNK, chans, LANES)
        peak = jnp.max(scores, axis=1, keepdims=True)
        raised = jnp.exp(scores - peak).astype(BF16).astype(F32)
        part_out[s, chunk, :, D : D + LANES] = jnp.max(scores, axis=1)
        part_out[s, chunk, :, D + LANES :] = jnp.sum(raised, axis=1)
        own = (iota(raised.shape, 2) & (COPIES - 1)) == (iota(raised.shape, 0) & (COPIES - 1))
        placed = jnp.where(own, raised, 0.0).reshape(CHUNK * chans, LANES)
        highs, lows = [], []
        for k in range(CHUNK // COPIES):
            rows = slice(k * span_rows, (k + 1) * span_rows)
            total = jnp.dot(placed[rows].T.astype(BF16), normed[rows], preferred_element_type=F32)
            high = total.astype(BF16)
            highs.append(high)
            lows.append((total - high.astype(F32)).astype(BF16))
        depth_n = WIDE // HEAD_DIM * COPIES
        head = lax.shift_right_logical(iota((COPIES, WIDE), 1), 6)
        for n in range(D // WIDE):
            rows = slice(n * depth_n, (n + 1) * depth_n)
            columns = slice(n * WIDE, (n + 1) * WIDE)
            mixed_heads = jnp.dot(
                jnp.concatenate([part[rows] for part in highs + lows], axis=0),
                wv[:, columns], preferred_element_type=F32,
            )
            for k in range(CHUNK // COPIES):
                low = (CHUNK // COPIES + k) * depth_n
                both = mixed_heads[k * depth_n : (k + 1) * depth_n] + mixed_heads[low : low + depth_n]
                kept = both[:COPIES]
                for h in range(1, WIDE // HEAD_DIM):
                    kept = jnp.where(head == h, both[h * COPIES : (h + 1) * COPIES], kept)
                part_out[s, chunk, k * COPIES : (k + 1) * COPIES, columns] = kept

    def step(s):
        order = [(my_chunk + 1 + i) % nchunks for i in range(nchunks)]
        wait_halo(s, first_of(order[0]))
        def prepare(i):
            wait_halo(s, rest_of(order[i]))
            if i + 1 < nchunks:
                wait_halo(s, first_of(order[i + 1]))

            @pl.when(order[i] == nchunks - 1)
            def _():
                patches[s, cols] = patches[s, 0]

        def finish(i):
            aggregate(s, order[i], i % 2)

            @pl.loop(0, owners)
            def _(a):
                to = order[i] * owners + a

                @pl.when(to != me)
                def _():
                    part_copy(s, to, me).start()

        for i in range(nchunks - 1):
            prepare(i)
            embed(s, order[i], i % 2)
            if i > 0:
                finish(i - 1)
        finish(nchunks - 2)
        prepare(nchunks - 1)
        embed(s, order[nchunks - 1], (nchunks - 1) % 2)
        finish(nchunks - 1)

        part_in[s, me] = part_out[s, my_chunk]

        @pl.when(s == 0)
        def _():
            wait_weight(3)

        @pl.loop(1, nchan)
        def _(i):
            peer = (me + i) % nchan
            part_copy(s, peer, me).wait_send()
            part_copy(s, peer, peer).wait_recv()

        peaks = part_in[s, :, :, D : D + LANES]
        factors = jnp.exp(peaks - jnp.max(peaks, axis=0)[None])
        total = jnp.sum(factors * part_in[s, :, :, D + LANES :], axis=0)
        factors = factors / total[None]
        factors = jnp.dot(
            split_parts(factors.reshape(nchan * CHUNK, LANES)), expand[...], preferred_element_type=F32
        ).reshape(nchan, CHUNK, D)
        blended = jnp.sum(factors * part_in[s, :, :, :D], axis=0).astype(BF16)
        mixed[s, my_chunk] = jnp.dot(blended, wo[...], preferred_element_type=F32).astype(BF16)

        @pl.loop(1, nchunks)
        def _(i):
            mixed_copy(s, (my_chunk + nchunks - i) % nchunks, my_chunk).start()

        @pl.when(s == 0)
        def _():
            remote_decoder(here_d).wait_send()
            remote_decoder(there_d).wait_recv()

        carry[...] = jnp.zeros_like(carry)

        @pl.loop(0, nchunks + LAG)
        def _(i):
            @pl.when(i < nchunks)
            def _():
                chunk = (my_chunk + i) % nchunks

                @pl.when(i > 0)
                def _():
                    mixed_copy(s, chunk, my_chunk).wait_send()
                    mixed_copy(s, chunk, chunk).wait_recv()

                rows = mixed[s, chunk].astype(F32)
                for j in range(CHUNK):
                    mixed_rows[j] = jnp.broadcast_to(rows[j : j + 1], (group, D))
                hidden = gelu(
                    mixed_rows[...][:, None] + de_ref[...].reshape(groups, group, D)[None]
                ).reshape(CHUNK * chans, D).astype(BF16)
                pixels = jnp.dot(hidden, wd[...], preferred_element_type=F32).reshape(CHUNK, chans, D)
                right = pixels[:, :, D // 2 :]
                blocks = pixels[:, :, : D // 2] + jnp.concatenate([carry[...][None], right[:-1]], axis=0)
                carry[...] = right[CHUNK - 1]
                rim_out[s, 0, chunk] = blocks[:, :, :LANES].astype(BF16)
                rim_out[s, 1, chunk] = blocks[:, :, 3 * LANES :].astype(BF16)

                @pl.when(has_up)
                def _():
                    rim_up(s, chunk).start()

                @pl.when(has_down)
                def _():
                    rim_down(s, chunk).start()

                state[places(chunk)] = state[places(chunk)] + blocks[:, :, LANES : 3 * LANES]

                @pl.when(i == nchunks - 1)
                def _():
                    edge_out[s, 0] = carry[:, :LANES].astype(BF16)
                    edge_out[s, 1] = carry[:, 3 * LANES :].astype(BF16)

                    @pl.when(has_up)
                    def _():
                        edge_up(s).start()

                    @pl.when(has_down)
                    def _():
                        edge_down(s).start()

                    state[seam] = state[seam] + carry[:, LANES : 3 * LANES]

            @pl.when(i >= LAG)
            def _():
                chunk = (my_chunk + i - LAG) % nchunks

                @pl.when(has_up)
                def _():
                    rim_up(s, chunk).wait_send()
                    rim_down(s, chunk).wait_recv()
                    state[places(chunk), :, :LANES] = (
                        state[places(chunk), :, :LANES] + rim_in[s, 0, chunk].astype(F32)
                    )

                @pl.when(has_down)
                def _():
                    rim_down(s, chunk).wait_send()
                    rim_up(s, chunk).wait_recv()
                    state[places(chunk), :, LANES:] = (
                        state[places(chunk), :, LANES:] + rim_in[s, 1, chunk].astype(F32)
                    )

                @pl.when(s < STEPS - 1)
                def _():
                    patches[s + 1, places(chunk), :, LANES : 3 * LANES] = state[places(chunk)].astype(BF16)

                    @pl.when(i == LAG)
                    def _():
                        send_halo(s + 1, rest_of(my_chunk))

                    @pl.when(i > LAG)
                    def _():
                        send_halo(s + 1, first_of(chunk))
                        send_halo(s + 1, rest_of(chunk))

                @pl.when(s == STEPS - 1)
                def _():
                    @pl.when(i == LAG)
                    def _():
                        store(my_chunk, seam + 1, CHUNK - 1).start()

                    @pl.when(i > LAG)
                    def _():
                        store(chunk, chunk * CHUNK, CHUNK).start()

        @pl.when(has_up)
        def _():
            edge_up(s).wait_send()
            edge_down(s).wait_recv()
            state[seam, :, :LANES] = state[seam, :, :LANES] + edge_in[s, 0].astype(F32)

        @pl.when(has_down)
        def _():
            edge_down(s).wait_send()
            edge_up(s).wait_recv()
            state[seam, :, LANES:] = state[seam, :, LANES:] + edge_in[s, 1].astype(F32)

        @pl.when(s < STEPS - 1)
        def _():
            patches[s + 1, seam, :, LANES : 3 * LANES] = state[seam].astype(BF16)
            send_halo(s + 1, first_of(my_chunk))

    @pl.loop(0, STEPS)
    def _(s):
        step(s)

    store(nchunks, seam, 1).start()
    store(my_chunk, seam + 1, CHUNK - 1).wait()
    for i in range(1, nchunks):
        chunk = (my_chunk + i) % nchunks
        store(chunk, chunk * CHUNK, CHUNK).wait()
    store(nchunks, seam, 1).wait()


def lay_kernel(chans, cols, blocks_ref, out_ref, held, pixels_out, in_sem, out_sem):
    group = min(8, chans)
    groups = chans // group
    tiles_across = cols // 8

    def load(g):
        return pltpu.make_async_copy(
            blocks_ref.at[:, pl.ds(pl.multiple_of(g * group, group), group)], held.at[g], in_sem.at[g]
        )

    def store(g, t):
        rows = pl.ds(pl.multiple_of(g * (group * STRIDE), group * STRIDE), group * STRIDE)
        return pltpu.make_async_copy(
            pixels_out.at[t, rows], out_ref.at[rows, t * LANES : (t + 1) * LANES], out_sem.at[g, t]
        )

    load(0).start()

    @pl.loop(0, groups)
    def _(g):
        load(g).wait()

        @pl.when(g + 1 < groups)
        def _():
            load(g + 1).start()

        @pl.loop(0, 2)
        def _(half):
            first = g * (group * STRIDE) + half * 8
            there = pl.ds(pl.multiple_of(half * LANES, LANES), LANES)
            columns = [
                trade_chunks([held[g, t * 8 + j, :, there] for j in range(8)]) for t in range(cols // 8)
            ]
            for r in range(8):
                field = jnp.concatenate([tiles[r] for tiles in columns], axis=1)
                field = pltpu.roll(field, field.shape[1] - RIM, 1)
                for t in range(tiles_across):
                    pixels_out[t, pl.ds(first + r, group, stride=STRIDE), :] = field[
                        :, t * LANES : (t + 1) * LANES
                    ]

        for t in range(tiles_across):
            store(g, t).start()

    @pl.loop(0, groups)
    def _(g):
        for t in range(tiles_across):
            store(g, t).wait()


def body(mesh_sizes, state_field, patch_weight, chan_embed, query_keys, value_weight, out_weight, dec_embed, dec_weight):
    nchan, nband, nrep = mesh_sizes
    chans, rows, width = state_field.shape
    cols = width // STRIDE
    group = min(8, chans)
    groups = chans // group
    nchunks = cols // CHUNK
    assert rows == STRIDE and nrep == 2 and nchan % nchunks == 0
    vmem = pl.BlockSpec(memory_space=pltpu.VMEM)
    whole = pl.BlockSpec(memory_space=pl.ANY)
    dma = pltpu.SemaphoreType.DMA
    blocks = pl.pallas_call(
        functools.partial(kernel, (chans, cols, nchan, nband, nrep)),
        out_shape=jax.ShapeDtypeStruct((cols, chans, 2 * LANES), F32),
        in_specs=[whole, whole, vmem, vmem, whole, whole, vmem, vmem],
        out_specs=whole,
        scratch_shapes=[
            pltpu.VMEM((cols, chans, 2 * LANES), F32),
            pltpu.VMEM((STEPS, cols + 1, chans, D // 2), BF16),
            pltpu.VMEM((2, PATCH, STRIDE, D), BF16),
            pltpu.VMEM((D, D), BF16),
            pltpu.VMEM((D, D), BF16),
            pltpu.VMEM((D, D), BF16),
            pltpu.VMEM((LANES, D), BF16),
            pltpu.VMEM((LANES, D), BF16),
            pltpu.VMEM((CHUNK, group, D), F32),
            pltpu.VMEM((cols // 8, chans * rows, LANES), F32),
            pltpu.VMEM((STEPS, 2, nchunks, CHUNK, chans, LANES), BF16),
            pltpu.VMEM((STEPS, 2, nchunks, CHUNK, chans, LANES), BF16),
            pltpu.VMEM((STEPS, 2, chans, LANES), BF16),
            pltpu.VMEM((STEPS, 2, chans, LANES), BF16),
            pltpu.VMEM((chans, D // 2), F32),
            pltpu.VMEM((STEPS, nchunks, CHUNK, PACKET), F32),
            pltpu.VMEM((STEPS, nchan, CHUNK, PACKET), F32),
            pltpu.VMEM((STEPS, nchunks, CHUNK, D), BF16),
            pltpu.VMEM((CHUNK * chans, D), BF16),
            pltpu.VMEM((CHUNK * chans, D), BF16),
            pltpu.VMEM((CHUNK * chans, D), BF16),
            dma((cols // 8,)), dma((nchunks + 1,)), dma((4,)), dma((5,)), dma((5,)),
            dma((STEPS, 2, 2 * nchunks)), dma((STEPS, 2, 2 * nchunks)),
            dma((STEPS, 2, nchunks + 1)), dma((STEPS, 2, nchunks + 1)),
            dma((STEPS, nchan)), dma((STEPS, nchan)),
            dma((STEPS, nchunks)), dma((STEPS, nchunks)),
        ],
        compiler_params=pltpu.CompilerParams(
            collective_id=0, has_side_effects=True, vmem_limit_bytes=60 * 1024 * 1024
        ),
        name="rollout",
    )(
        state_field.reshape(chans * rows, width),
        patch_weight.reshape(PATCH // nrep, 2, STRIDE, D),
        chan_embed,
        query_keys.T,
        value_weight,
        out_weight,
        dec_embed,
        dec_weight,
    )
    return pl.pallas_call(
        functools.partial(lay_kernel, chans, cols),
        out_shape=jax.ShapeDtypeStruct((chans * rows, width), F32),
        in_specs=[whole],
        out_specs=whole,
        scratch_shapes=[
            pltpu.VMEM((groups, cols, group, 2 * LANES), F32),
            pltpu.VMEM((cols // 8, chans * rows, LANES), F32),
            dma((groups,)), dma((groups, cols // 8)),
        ],
        compiler_params=pltpu.CompilerParams(vmem_limit_bytes=60 * 1024 * 1024),
        name="lay",
    )(blocks).reshape(state_field.shape)


def solution(mesh):
    in_specs = (
        P(("groups", "chan"), ("band", "rep"), None),
        P("rep", None),
        P("chan", None),
        P(),
        P("rep", None),
        P("rep", None),
        P("chan", None),
        P("rep", None),
    )
    out_specs = P(("groups", "chan"), ("band", "rep"), None)
    sizes = (mesh.shape["chan"], mesh.shape["band"], mesh.shape["rep"])
    return jax.shard_map(
        functools.partial(body, sizes), mesh=mesh, in_specs=in_specs, out_specs=out_specs, check_vma=False
    )
```

```python
import functools

import jax
import jax.numpy as jnp
from jax import lax
from jax.experimental import pallas as pl
from jax.experimental.pallas import tpu as pltpu
from jax.sharding import PartitionSpec as P

D = 1024
HEADS = 16
HEAD_DIM = D // HEADS
PATCH = 32
STRIDE = 16
RIM = 8
STEPS = 2
LANES = 128
COPIES = LANES // HEADS
CHUNK = 16
WIDE = 256
LAG = 3
MESH = pl.DeviceIdType.MESH
F32 = jnp.float32
BF16 = jnp.bfloat16


def iota(shape, dim):
    return lax.broadcasted_iota(jnp.int32, shape, dim)


def swap_chunks(tiles):
    tiles = list(tiles)
    chunk = lax.shift_right_logical(iota(tiles[0].shape, 1), 4)
    for bit in (1, 2, 4):
        high = (chunk & bit) != 0
        for low in range(8):
            if low & bit:
                continue
            first, second = tiles[low], tiles[low + bit]
            if bit == 4:
                moved = pltpu.roll(jnp.where(high, first, second), LANES // 2, 1)
                tiles[low] = jnp.where(high, moved, first)
                tiles[low + bit] = jnp.where(high, second, moved)
                continue
            tiles[low] = jnp.where(high, pltpu.roll(second, 16 * bit, 1), first)
            tiles[low + bit] = jnp.where(high, second, pltpu.roll(first, LANES - 16 * bit, 1))
    return tiles


def trade_chunks(tiles):
    tiles = list(tiles)
    lane = iota(tiles[0].shape, 1)
    chunk = lax.shift_right_logical(lane, 4)
    for bit in (1, 2, 4):
        high = (chunk & bit) != 0
        for low in range(8):
            if low & bit:
                continue
            first, second = tiles[low], tiles[low + bit]
            moved = jnp.where(high, first, second)
            if bit == 4:
                moved = pltpu.roll(moved, LANES // 2, 1)
            else:
                moved = jnp.take_along_axis(moved, lane ^ (16 * bit), axis=1)
            tiles[low] = jnp.where(high, moved, first)
            tiles[low + bit] = jnp.where(high, second, moved)
    return tiles


def split_parts(values):
    high = values.astype(BF16)
    rest = values - high.astype(F32)
    middle = rest.astype(BF16)
    low = (rest - middle.astype(F32)).astype(BF16)
    copy = iota(values.shape, values.ndim - 1) & (COPIES - 1)
    parts = jnp.where(copy == 0, high.astype(F32), jnp.where(copy == 1, middle.astype(F32), low.astype(F32)))
    return jnp.where(copy < 3, parts, 0.0).astype(BF16)


def normalize(tokens):
    centre = jnp.mean(tokens, axis=-1, keepdims=True)
    moved = tokens - centre
    spread = jnp.mean(jnp.square(moved), axis=-1, keepdims=True)
    return (moved * lax.rsqrt(spread + 1e-05)).astype(BF16)


def gelu(x):
    return 0.5 * x * (1.0 + lax.erf(x * 0.7071067811865476))


def kernel(
    sizes,
    x_ref, pw_ref, ce_ref, qk_ref, vw_ref, ow_ref, de_ref, dw_ref,
    out_ref,
    state, patches, wp, wv, wo, wd, expand, keys, mixed_rows,
    pixels_in, rim_out, rim_in, edge_out, edge_in, carry, part_out, part_in, tops_out, tops_in, mixed,
    tokens_a, tokens_b, normed,
    x_sem, out_sem, w_local, w_send, w_recv, h_send, h_recv, r_send, r_recv, p_send, p_recv, t_send, t_recv, m_send, m_recv,
):
    chans, cols, nchan, nband, nrep = sizes
    tokens = (tokens_a, tokens_b)
    group = min(8, chans)
    groups = chans // group
    pack = min(16, chans)
    ratio = pack // group
    packs = chans // pack
    nchunks = cols // CHUNK
    owners = nchan // nchunks
    me = lax.axis_index("chan")
    rep = lax.axis_index("rep")
    place = lax.axis_index("band") * nrep + rep
    last = nband * nrep - 1
    has_up = place > 0
    has_down = place < last
    up_place = jnp.maximum(place - 1, 0)
    down_place = jnp.minimum(place + 1, last)
    up = {"band": up_place // nrep, "rep": up_place % nrep}
    down = {"band": down_place // nrep, "rep": down_place % nrep}
    my_chunk = me // owners
    my_lane = me % owners

    tiles_across = cols // 8

    def load(t):
        return pltpu.make_async_copy(
            x_ref.at[:, t * LANES : (t + 1) * LANES], pixels_in.at[t], x_sem.at[t]
        )

    for t in range(tiles_across):
        load(t).start()

    barrier = pltpu.get_barrier_semaphore()

    @pl.when(has_up)
    def _():
        pl.semaphore_signal(barrier, inc=1, device_id=up, device_id_type=MESH)

    @pl.when(has_down)
    def _():
        pl.semaphore_signal(barrier, inc=1, device_id=down, device_id_type=MESH)

    @pl.loop(1, nchan)
    def _(i):
        pl.semaphore_signal(
            barrier, inc=1, device_id={"chan": (me + i) % nchan}, device_id_type=MESH
        )

    pl.semaphore_wait(
        barrier, nchan - 1 + jnp.minimum(place, 1) + jnp.minimum(last - place, 1)
    )

    other = {"rep": 1 - rep}
    depth = D // nrep
    rows_r = PATCH // nrep
    here_r = pl.ds(pl.multiple_of(rep * rows_r, rows_r), rows_r)
    here_d = pl.ds(pl.multiple_of(rep * depth, depth), depth)
    there_r = pl.ds(pl.multiple_of((1 - rep) * rows_r, rows_r), rows_r)
    there_d = pl.ds(pl.multiple_of((1 - rep) * depth, depth), depth)
    moves = [
        (pw_ref.at[:, 0], lambda rows, _: wp.at[0, rows]),
        (pw_ref.at[:, 1], lambda rows, _: wp.at[1, rows]),
        (vw_ref, lambda _, rows: wv.at[rows]),
        (ow_ref, lambda _, rows: wo.at[rows]),
    ]

    def local_weight(n):
        source, target = moves[n]
        return pltpu.make_async_copy(source, target(here_r, here_d), w_local.at[n])

    def remote_weight(n, rows_r_, rows_d_):
        source, target = moves[n]
        return pltpu.make_async_remote_copy(
            src_ref=source, dst_ref=target(rows_r_, rows_d_),
            send_sem=w_send.at[n], recv_sem=w_recv.at[n],
            device_id=other, device_id_type=MESH,
        )

    def remote_decoder(rows):
        return pltpu.make_async_remote_copy(
            src_ref=wd.at[rows], dst_ref=wd.at[rows],
            send_sem=w_send.at[len(moves)], recv_sem=w_recv.at[len(moves)],
            device_id=other, device_id_type=MESH,
        )

    for n in range(len(moves)):
        local_weight(n).start()
        remote_weight(n, here_r, here_d).start()

    def wait_weight(n):
        local_weight(n).wait()
        remote_weight(n, here_r, here_d).wait_send()
        remote_weight(n, there_r, there_d).wait_recv()

    lane = iota((LANES, D), 0)
    feature = lax.shift_right_logical(iota((LANES, D), 1), 6)
    expand[...] = jnp.where(
        (lax.shift_right_logical(lane, 3) == feature) & ((lane & (COPIES - 1)) < 3), 1.0, 0.0
    ).astype(BF16)

    def span(g):
        return pl.ds(pl.multiple_of(g * group, group), group)

    def bundle(p):
        return pl.ds(pl.multiple_of(p * pack, pack), pack)

    def places(p):
        return pl.ds(pl.multiple_of(p * CHUNK, CHUNK), CHUNK)

    every = pl.ds(0, chans)

    def halo_up(s, n, first, count, which=every):
        return pltpu.make_async_remote_copy(
            src_ref=patches.at[s, pl.ds(first, count), which, LANES : 2 * LANES],
            dst_ref=patches.at[s, pl.ds(first, count), which, 3 * LANES :],
            send_sem=h_send.at[s, 0, n], recv_sem=h_recv.at[s, 1, n],
            device_id=up, device_id_type=MESH,
        )

    def halo_down(s, n, first, count, which=every):
        return pltpu.make_async_remote_copy(
            src_ref=patches.at[s, pl.ds(first, count), which, 2 * LANES : 3 * LANES],
            dst_ref=patches.at[s, pl.ds(first, count), which, :LANES],
            send_sem=h_send.at[s, 1, n], recv_sem=h_recv.at[s, 0, n],
            device_id=down, device_id_type=MESH,
        )

    def rim_up(s, n):
        return pltpu.make_async_remote_copy(
            src_ref=rim_out.at[s, 0, n], dst_ref=rim_in.at[s, 1, n],
            send_sem=r_send.at[s, 0, n], recv_sem=r_recv.at[s, 1, n],
            device_id=up, device_id_type=MESH,
        )

    def rim_down(s, n):
        return pltpu.make_async_remote_copy(
            src_ref=rim_out.at[s, 1, n], dst_ref=rim_in.at[s, 0, n],
            send_sem=r_send.at[s, 1, n], recv_sem=r_recv.at[s, 0, n],
            device_id=down, device_id_type=MESH,
        )

    def edge_up(s):
        return pltpu.make_async_remote_copy(
            src_ref=edge_out.at[s, 0], dst_ref=edge_in.at[s, 1],
            send_sem=r_send.at[s, 0, nchunks], recv_sem=r_recv.at[s, 1, nchunks],
            device_id=up, device_id_type=MESH,
        )

    def edge_down(s):
        return pltpu.make_async_remote_copy(
            src_ref=edge_out.at[s, 1], dst_ref=edge_in.at[s, 0],
            send_sem=r_send.at[s, 1, nchunks], recv_sem=r_recv.at[s, 0, nchunks],
            device_id=down, device_id_type=MESH,
        )

    seam = my_chunk * CHUNK

    def fill_own(s, p):
        patches[s, pl.ds(0, cols), bundle(p), LANES : 3 * LANES] = state[:, bundle(p), :].astype(BF16)

    def first_of(chunk):
        return 2 * chunk, chunk * CHUNK, 1

    def rest_of(chunk):
        return 2 * chunk + 1, chunk * CHUNK + 1, CHUNK - 1

    def send_halo(s, piece, which=every):
        @pl.when(has_up)
        def _():
            halo_up(s, *piece, which).start()

        @pl.when(has_down)
        def _():
            halo_down(s, *piece, which).start()

    def wait_halo(s, piece):
        @pl.when(has_up)
        def _():
            halo_up(s, *piece).wait_send()
            halo_down(s, *piece).wait_recv()

        @pl.when(has_down)
        def _():
            halo_down(s, *piece).wait_send()
            halo_up(s, *piece).wait_recv()

    for t in range(tiles_across):
        load(t).wait()

    @pl.loop(0, packs)
    def _(p):
        @pl.loop(0, ratio)
        def _(i):
            g = p * ratio + i

            @pl.loop(0, 2)
            def _(half):
                first = g * (group * STRIDE) + half * 8
                fields = [
                    pltpu.roll(
                        jnp.concatenate(
                            [
                                pixels_in[t, pl.ds(first + r, group, stride=STRIDE), :]
                                for t in range(tiles_across)
                            ],
                            axis=1,
                        ),
                        RIM, 1,
                    )
                    for r in range(8)
                ]
                there = pl.ds(pl.multiple_of(half * LANES, LANES), LANES)
                for t in range(cols // 8):
                    tiles = trade_chunks([field[:, t * LANES : (t + 1) * LANES] for field in fields])
                    for j in range(8):
                        state[t * 8 + j, span(g), there] = tiles[j]

        fill_own(0, p)

        @pl.loop(0, nchunks)
        def _(i):
            chunk = (my_chunk + 1 + i) % nchunks
            send_halo(0, first_of(chunk), bundle(p))
            send_halo(0, rest_of(chunk), bundle(p))

    source = iota((2 * LANES, 2 * LANES), 0)
    target = iota((2 * LANES, 2 * LANES), 1)
    moved = (
        (lax.shift_right_logical(source, 4) & 1) * LANES
        + lax.shift_right_logical(source, 5) * STRIDE
        + (source & (STRIDE - 1))
    )
    order = jnp.where(moved == target, 1.0, 0.0).astype(BF16)
    for b in range(D // (2 * LANES)):
        ordered = jnp.dot(
            dw_ref[:, b * 2 * LANES : (b + 1) * 2 * LANES], order, preferred_element_type=F32
        )
        ordered = (0.25 * ordered).astype(BF16)
        wd[here_d, b * LANES : (b + 1) * LANES] = ordered[:, :LANES]
        wd[here_d, D // 2 + b * LANES : D // 2 + (b + 1) * LANES] = ordered[:, LANES:]
    remote_decoder(here_d).start()

    zeros = jnp.zeros((STEPS, cols, chans, LANES), BF16)

    @pl.when(jnp.logical_not(has_up))
    def _():
        patches[:, :cols, :, :LANES] = zeros

    @pl.when(jnp.logical_not(has_down))
    def _():
        patches[:, :cols, :, 3 * LANES :] = zeros

    spots = jnp.where(
        lax.shift_right_logical(iota((LANES, HEADS), 0), 3) == iota((LANES, HEADS), 1), 1.0, 0.0
    ).astype(BF16)
    keys[...] = jnp.dot(spots, qk_ref[...], preferred_element_type=F32).astype(BF16)

    for n in range(3):
        wait_weight(n)

    def part_copy(s, to, slot):
        return pltpu.make_async_remote_copy(
            src_ref=part_out.at[s, to // owners], dst_ref=part_in.at[s, slot],
            send_sem=p_send.at[s, to], recv_sem=p_recv.at[s, slot],
            device_id={"chan": to}, device_id_type=MESH,
        )

    def tops_copy(s, to, slot):
        return pltpu.make_async_remote_copy(
            src_ref=tops_out.at[s, to // owners], dst_ref=tops_in.at[s, slot],
            send_sem=t_send.at[s, to], recv_sem=t_recv.at[s, slot],
            device_id={"chan": to}, device_id_type=MESH,
        )

    def mixed_copy(s, chunk, slot):
        return pltpu.make_async_remote_copy(
            src_ref=mixed.at[s, my_chunk], dst_ref=mixed.at[s, slot],
            send_sem=m_send.at[s, chunk], recv_sem=m_recv.at[s, slot],
            device_id={"chan": chunk * owners + my_lane}, device_id_type=MESH,
        )

    def store(n, first, count):
        return pltpu.make_async_copy(
            state.at[pl.ds(first, count)], out_ref.at[pl.ds(first, count)], out_sem.at[n]
        )

    span_rows = COPIES * chans

    def embed(s, chunk, slot):
        start = pl.multiple_of(chunk * CHUNK, CHUNK)
        rows = jnp.concatenate(
            [patches[s, pl.ds(start, CHUNK)], patches[s, pl.ds(start + 1, CHUNK)]], axis=2
        ).reshape(CHUNK * chans, D)
        embedded = jnp.dot(rows, wp[...].reshape(D, D), preferred_element_type=F32)
        embedded = embedded.reshape(CHUNK, chans, D) + ce_ref[...][None]
        tokens[slot][...] = embedded.astype(BF16).reshape(CHUNK * chans, D)

    def aggregate(s, chunk, slot):
        for r in range(0, CHUNK * chans, 16):
            normed[r : r + 16] = normalize(tokens[slot][r : r + 16].astype(F32))
        scores = lax.dot_general(
            normed[...], keys[...], (((1,), (1,)), ((), ())), preferred_element_type=F32
        )
        scores = scores.reshape(CHUNK, chans, LANES)
        peak = jnp.max(scores, axis=1, keepdims=True)
        raised = jnp.exp(scores - peak).astype(BF16).astype(F32)
        tops_out[s, chunk, :, :LANES] = jnp.max(scores, axis=1)
        tops_out[s, chunk, :, LANES:] = jnp.sum(raised, axis=1)
        own = (iota(raised.shape, 2) & (COPIES - 1)) == (iota(raised.shape, 0) & (COPIES - 1))
        placed = jnp.where(own, raised, 0.0).reshape(CHUNK * chans, LANES)
        highs, lows = [], []
        for k in range(CHUNK // COPIES):
            rows = slice(k * span_rows, (k + 1) * span_rows)
            total = jnp.dot(placed[rows].T.astype(BF16), normed[rows], preferred_element_type=F32)
            high = total.astype(BF16)
            highs.append(high)
            lows.append((total - high.astype(F32)).astype(BF16))
        depth_n = WIDE // HEAD_DIM * COPIES
        head = lax.shift_right_logical(iota((COPIES, WIDE), 1), 6)
        for n in range(D // WIDE):
            rows = slice(n * depth_n, (n + 1) * depth_n)
            columns = slice(n * WIDE, (n + 1) * WIDE)
            mixed_heads = jnp.dot(
                jnp.concatenate([part[rows] for part in highs + lows], axis=0),
                wv[:, columns], preferred_element_type=F32,
            )
            kepts = []
            for k in range(CHUNK // COPIES):
                low = (CHUNK // COPIES + k) * depth_n
                both = mixed_heads[k * depth_n : (k + 1) * depth_n] + mixed_heads[low : low + depth_n]
                kept = both[:COPIES]
                for h in range(1, WIDE // HEAD_DIM):
                    kept = jnp.where(head == h, both[h * COPIES : (h + 1) * COPIES], kept)
                kepts.append(kept)
            part_out[s, chunk, :, columns] = jnp.concatenate(kepts, axis=0).astype(BF16)

    def step(s):
        order = [(my_chunk + 1 + i) % nchunks for i in range(nchunks)]
        wait_halo(s, first_of(order[0]))
        def prepare(i):
            wait_halo(s, rest_of(order[i]))
            if i + 1 < nchunks:
                wait_halo(s, first_of(order[i + 1]))

            @pl.when(order[i] == nchunks - 1)
            def _():
                patches[s, cols] = patches[s, 0]

        def finish(i):
            aggregate(s, order[i], i % 2)

            @pl.loop(0, owners)
            def _(a):
                to = order[i] * owners + a

                @pl.when(to != me)
                def _():
                    part_copy(s, to, me).start()
                    tops_copy(s, to, me).start()

        for i in range(nchunks - 1):
            prepare(i)
            embed(s, order[i], i % 2)
            if i > 0:
                finish(i - 1)
        finish(nchunks - 2)
        prepare(nchunks - 1)
        embed(s, order[nchunks - 1], (nchunks - 1) % 2)
        finish(nchunks - 1)

        part_in[s, me] = part_out[s, my_chunk]
        tops_in[s, me] = tops_out[s, my_chunk]

        @pl.when(s == 0)
        def _():
            wait_weight(3)

        @pl.loop(1, nchan)
        def _(i):
            peer = (me + i) % nchan
            part_copy(s, peer, me).wait_send()
            part_copy(s, peer, peer).wait_recv()
            tops_copy(s, peer, me).wait_send()
            tops_copy(s, peer, peer).wait_recv()

        peaks = tops_in[s, :, :, :LANES]
        factors = jnp.exp(peaks - jnp.max(peaks, axis=0)[None])
        total = jnp.sum(factors * tops_in[s, :, :, LANES:], axis=0)
        factors = factors / total[None]
        factors = jnp.dot(
            split_parts(factors.reshape(nchan * CHUNK, LANES)), expand[...], preferred_element_type=F32
        ).reshape(nchan, CHUNK, D)
        blended = jnp.sum(factors * part_in[s].astype(F32), axis=0).astype(BF16)
        mixed[s, my_chunk] = jnp.dot(blended, wo[...], preferred_element_type=F32).astype(BF16)

        @pl.loop(1, nchunks)
        def _(i):
            mixed_copy(s, (my_chunk + nchunks - i) % nchunks, my_chunk).start()

        @pl.when(s == 0)
        def _():
            remote_decoder(here_d).wait_send()
            remote_decoder(there_d).wait_recv()

        carry[...] = jnp.zeros_like(carry)

        @pl.loop(0, nchunks + LAG)
        def _(i):
            @pl.when(i < nchunks)
            def _():
                chunk = (my_chunk + i) % nchunks

                @pl.when(i > 0)
                def _():
                    mixed_copy(s, chunk, my_chunk).wait_send()
                    mixed_copy(s, chunk, chunk).wait_recv()

                rows = mixed[s, chunk].astype(F32)
                for j in range(CHUNK):
                    mixed_rows[j] = jnp.broadcast_to(rows[j : j + 1], (group, D))
                hidden = gelu(
                    mixed_rows[...][:, None] + de_ref[...].reshape(groups, group, D)[None]
                ).reshape(CHUNK * chans, D).astype(BF16)
                pixels = jnp.dot(hidden, wd[...], preferred_element_type=F32).reshape(CHUNK, chans, D)
                right = pixels[:, :, D // 2 :]
                blocks = pixels[:, :, : D // 2] + jnp.concatenate([carry[...][None], right[:-1]], axis=0)
                carry[...] = right[CHUNK - 1]
                rim_out[s, 0, chunk] = blocks[:, :, :LANES].astype(BF16)
                rim_out[s, 1, chunk] = blocks[:, :, 3 * LANES :].astype(BF16)

                @pl.when(has_up)
                def _():
                    rim_up(s, chunk).start()

                @pl.when(has_down)
                def _():
                    rim_down(s, chunk).start()

                state[places(chunk)] = state[places(chunk)] + blocks[:, :, LANES : 3 * LANES]

                @pl.when(i == nchunks - 1)
                def _():
                    edge_out[s, 0] = carry[:, :LANES].astype(BF16)
                    edge_out[s, 1] = carry[:, 3 * LANES :].astype(BF16)

                    @pl.when(has_up)
                    def _():
                        edge_up(s).start()

                    @pl.when(has_down)
                    def _():
                        edge_down(s).start()

                    state[seam] = state[seam] + carry[:, LANES : 3 * LANES]

            @pl.when(i >= LAG)
            def _():
                chunk = (my_chunk + i - LAG) % nchunks

                @pl.when(has_up)
                def _():
                    rim_up(s, chunk).wait_send()
                    rim_down(s, chunk).wait_recv()
                    state[places(chunk), :, :LANES] = (
                        state[places(chunk), :, :LANES] + rim_in[s, 0, chunk].astype(F32)
                    )

                @pl.when(has_down)
                def _():
                    rim_down(s, chunk).wait_send()
                    rim_up(s, chunk).wait_recv()
                    state[places(chunk), :, LANES:] = (
                        state[places(chunk), :, LANES:] + rim_in[s, 1, chunk].astype(F32)
                    )

                @pl.when(s < STEPS - 1)
                def _():
                    patches[s + 1, places(chunk), :, LANES : 3 * LANES] = state[places(chunk)].astype(BF16)

                    @pl.when(i == LAG)
                    def _():
                        send_halo(s + 1, rest_of(my_chunk))

                    @pl.when(i > LAG)
                    def _():
                        send_halo(s + 1, first_of(chunk))
                        send_halo(s + 1, rest_of(chunk))

                @pl.when(s == STEPS - 1)
                def _():
                    @pl.when(i == LAG)
                    def _():
                        store(my_chunk, seam + 1, CHUNK - 1).start()

                    @pl.when(i > LAG)
                    def _():
                        store(chunk, chunk * CHUNK, CHUNK).start()

        @pl.when(has_up)
        def _():
            edge_up(s).wait_send()
            edge_down(s).wait_recv()
            state[seam, :, :LANES] = state[seam, :, :LANES] + edge_in[s, 0].astype(F32)

        @pl.when(has_down)
        def _():
            edge_down(s).wait_send()
            edge_up(s).wait_recv()
            state[seam, :, LANES:] = state[seam, :, LANES:] + edge_in[s, 1].astype(F32)

        @pl.when(s < STEPS - 1)
        def _():
            patches[s + 1, seam, :, LANES : 3 * LANES] = state[seam].astype(BF16)
            send_halo(s + 1, first_of(my_chunk))

    @pl.loop(0, STEPS)
    def _(s):
        step(s)

    store(nchunks, seam, 1).start()
    store(my_chunk, seam + 1, CHUNK - 1).wait()
    for i in range(1, nchunks):
        chunk = (my_chunk + i) % nchunks
        store(chunk, chunk * CHUNK, CHUNK).wait()
    store(nchunks, seam, 1).wait()


def lay_kernel(chans, cols, blocks_ref, out_ref, held, pixels_out, in_sem, out_sem):
    group = min(8, chans)
    groups = chans // group
    tiles_across = cols // 8

    def load(g, half):
        return pltpu.make_async_copy(
            blocks_ref.at[
                :, pl.ds(pl.multiple_of(g * group, group), group),
                pl.ds(pl.multiple_of(half * LANES, LANES), LANES),
            ],
            held.at[g, half], in_sem.at[g, half],
        )

    def store(g, t):
        rows = pl.ds(pl.multiple_of(g * (group * STRIDE), group * STRIDE), group * STRIDE)
        return pltpu.make_async_copy(
            pixels_out.at[t, rows], out_ref.at[rows, t * LANES : (t + 1) * LANES], out_sem.at[g, t]
        )

    load(0, 0).start()
    load(0, 1).start()

    @pl.loop(0, groups)
    def _(g):
        @pl.loop(0, 2)
        def _(half):
            load(g, half).wait()

            @pl.when(g + 1 < groups)
            def _():
                load(g + 1, half).start()

            first = g * (group * STRIDE) + half * 8
            columns = [
                trade_chunks([held[g, half, t * 8 + j] for j in range(8)]) for t in range(cols // 8)
            ]
            for r in range(8):
                field = jnp.concatenate([tiles[r] for tiles in columns], axis=1)
                field = pltpu.roll(field, field.shape[1] - RIM, 1)
                for t in range(tiles_across):
                    pixels_out[t, pl.ds(first + r, group, stride=STRIDE), :] = field[
                        :, t * LANES : (t + 1) * LANES
                    ]

        for t in range(tiles_across):
            store(g, t).start()

    @pl.loop(0, groups)
    def _(g):
        for t in range(tiles_across):
            store(g, t).wait()


def body(mesh_sizes, state_field, patch_weight, chan_embed, query_keys, value_weight, out_weight, dec_embed, dec_weight):
    nchan, nband, nrep = mesh_sizes
    chans, rows, width = state_field.shape
    cols = width // STRIDE
    group = min(8, chans)
    groups = chans // group
    nchunks = cols // CHUNK
    assert rows == STRIDE and nrep == 2 and nchan % nchunks == 0
    vmem = pl.BlockSpec(memory_space=pltpu.VMEM)
    whole = pl.BlockSpec(memory_space=pl.ANY)
    dma = pltpu.SemaphoreType.DMA
    blocks = pl.pallas_call(
        functools.partial(kernel, (chans, cols, nchan, nband, nrep)),
        out_shape=jax.ShapeDtypeStruct((cols, chans, 2 * LANES), F32),
        in_specs=[whole, whole, vmem, vmem, whole, whole, vmem, vmem],
        out_specs=whole,
        scratch_shapes=[
            pltpu.VMEM((cols, chans, 2 * LANES), F32),
            pltpu.VMEM((STEPS, cols + 1, chans, D // 2), BF16),
            pltpu.VMEM((2, PATCH, STRIDE, D), BF16),
            pltpu.VMEM((D, D), BF16),
            pltpu.VMEM((D, D), BF16),
            pltpu.VMEM((D, D), BF16),
            pltpu.VMEM((LANES, D), BF16),
            pltpu.VMEM((LANES, D), BF16),
            pltpu.VMEM((CHUNK, group, D), F32),
            pltpu.VMEM((cols // 8, chans * rows, LANES), F32),
            pltpu.VMEM((STEPS, 2, nchunks, CHUNK, chans, LANES), BF16),
            pltpu.VMEM((STEPS, 2, nchunks, CHUNK, chans, LANES), BF16),
            pltpu.VMEM((STEPS, 2, chans, LANES), BF16),
            pltpu.VMEM((STEPS, 2, chans, LANES), BF16),
            pltpu.VMEM((chans, D // 2), F32),
            pltpu.VMEM((STEPS, nchunks, CHUNK, D), BF16),
            pltpu.VMEM((STEPS, nchan, CHUNK, D), BF16),
            pltpu.VMEM((STEPS, nchunks, CHUNK, 2 * LANES), F32),
            pltpu.VMEM((STEPS, nchan, CHUNK, 2 * LANES), F32),
            pltpu.VMEM((STEPS, nchunks, CHUNK, D), BF16),
            pltpu.VMEM((CHUNK * chans, D), BF16),
            pltpu.VMEM((CHUNK * chans, D), BF16),
            pltpu.VMEM((CHUNK * chans, D), BF16),
            dma((cols // 8,)), dma((nchunks + 1,)), dma((4,)), dma((5,)), dma((5,)),
            dma((STEPS, 2, 2 * nchunks)), dma((STEPS, 2, 2 * nchunks)),
            dma((STEPS, 2, nchunks + 1)), dma((STEPS, 2, nchunks + 1)),
            dma((STEPS, nchan)), dma((STEPS, nchan)), dma((STEPS, nchan)), dma((STEPS, nchan)),
            dma((STEPS, nchunks)), dma((STEPS, nchunks)),
        ],
        compiler_params=pltpu.CompilerParams(
            collective_id=0, has_side_effects=True, vmem_limit_bytes=60 * 1024 * 1024
        ),
        name="rollout",
    )(
        state_field.reshape(chans * rows, width),
        patch_weight.reshape(PATCH // nrep, 2, STRIDE, D),
        chan_embed,
        query_keys.T,
        value_weight,
        out_weight,
        dec_embed,
        dec_weight,
    )
    return pl.pallas_call(
        functools.partial(lay_kernel, chans, cols),
        out_shape=jax.ShapeDtypeStruct((chans * rows, width), F32),
        in_specs=[whole],
        out_specs=whole,
        scratch_shapes=[
            pltpu.VMEM((groups, 2, cols, group, LANES), F32),
            pltpu.VMEM((cols // 8, chans * rows, LANES), F32),
            dma((groups, 2)), dma((groups, cols // 8)),
        ],
        compiler_params=pltpu.CompilerParams(vmem_limit_bytes=60 * 1024 * 1024),
        name="lay",
    )(blocks).reshape(state_field.shape)


def solution(mesh):
    in_specs = (
        P(("groups", "chan"), ("band", "rep"), None),
        P("rep", None),
        P("chan", None),
        P(),
        P("rep", None),
        P("rep", None),
        P("chan", None),
        P("rep", None),
    )
    out_specs = P(("groups", "chan"), ("band", "rep"), None)
    sizes = (mesh.shape["chan"], mesh.shape["band"], mesh.shape["rep"])
    return jax.shard_map(
        functools.partial(body, sizes), mesh=mesh, in_specs=in_specs, out_specs=out_specs, check_vma=False
    )
```
